1024 devices in a mesh: grp: 16 (over x, y), dev: 64 (over z, core).
Axes of the slice: x: 4, y: 4, z: 32, core: 2. Of those that a mesh axis runs over, the one named last changes fastest.
Arguments:
- queries: bfloat16 [1024, 3072], P(('grp', 'dev')), may hold values from -480 to 480
- cached_key_rows: bfloat16 [1024, 512, 512], P(('grp', 'dev')), may hold values from -6 to 6
- cached_value_rows: bfloat16 [1024, 512, 512], P(('grp', 'dev')), may hold values from -6 to 6
- incoming_keys: bfloat16 [1024, 512], P(('grp', 'dev')), may hold values from -6 to 6
- incoming_values: bfloat16 [1024, 512], P(('grp', 'dev')), may hold values from -6 to 6
- lengths: int32 [512], P('grp'), may hold values from 64 to 512, as said below
- residual: bfloat16 [512, 6144], P('grp'), may hold values from -6 to 6
- norm_gain: float32 [6144], replicated, may hold values from 0.25 to 1.75
- expert_ids: int32 [512, 2], P('grp'), may hold values from 0 to 7, all different within a row; in each aligned block of 32 rows (0 to 31, 32 to 63, ...) at most 10 rows name the same one
- route_logits: float32 [512, 2], P('grp'), may hold values from -6 to 6
- w_gate: bfloat16 [6144, 65536], P(None, ('dev', 'grp')), may hold values from -0.078125 to 0.078125
- w_up: bfloat16 [6144, 65536], P(None, ('dev', 'grp')), may hold values from -0.078125 to 0.078125
- w_down: bfloat16 [65536, 6144], P(('dev', 'grp')), may hold values from -0.0625 to 0.0625
Outputs:
- moe_out: bfloat16 [512, 6144], P('grp', 'dev')
The draws below stay inside these ranges and needn't reach their ends.
Inputs may be any that keep to these rules, and one draw needn't show every extreme that they name: `lengths`: A sequence has at least 64 live positions; some sequence has exactly 512. `expert_ids`: each token names 2 different experts; among the tokens of one group (32 aligned rows) no expert is named more than 10 times, a bound that some block reaches.
All inputs are finite; a program needn't handle non-finite values.
Results may differ from the reference program's by a relative error of at most 0.007.
Values may be sent and summed in bfloat16 or wider, within the bound.
A program may use at most 32 MiB of HBM per device.

```python
import math
import jax
import jax.numpy as jnp
import numpy as np
from jax import lax

D = 6144
QUERY_HEADS = 48
KEY_VALUE_HEADS = 8
HEAD_SIZE = 128
E = 8
FF = 8192
TOPK = 2
SHARING_DEVICES = 2
CACHED_POSITIONS = 512
TOK_GRP = 32
TOTAL_SEQUENCES = 512
ROWCAP = 10
N_GRP = 16


def draw_queries(key, part):
    first_key = jax.random.fold_in(key, 0)
    values = jnp.clip(jax.random.normal(first_key, (TOTAL_SEQUENCES * SHARING_DEVICES, QUERY_HEADS // SHARING_DEVICES, HEAD_SIZE), jnp.float32), -6.0, 6.0)
    return values.reshape(TOTAL_SEQUENCES * SHARING_DEVICES, D // SHARING_DEVICES).astype(jnp.bfloat16)


def draw_lengths(key, part):
    first_key, second_key = jax.random.split(key)
    drawn = jax.random.randint(first_key, (TOTAL_SEQUENCES,), CACHED_POSITIONS // 8, CACHED_POSITIONS + 1, jnp.int32)
    longest = jax.random.randint(second_key, (), 0, TOTAL_SEQUENCES, jnp.int32)
    return jnp.where(jnp.arange(TOTAL_SEQUENCES, dtype=jnp.int32) == longest, CACHED_POSITIONS, drawn).astype(jnp.int32)


def levels(key, shape, shards, low, top_value):
    def one(dim, shards_of):
        draws = jax.random.uniform(jax.random.fold_in(jax.random.fold_in(key, 6), dim), (shards_of,), jnp.float32, low / len(shards), top_value / len(shards))
        return jnp.repeat(jnp.exp(draws), shape[dim] // shards_of).reshape((-1,) + (1,) * (len(shape) - dim - 1))

    gain = one(*shards[0])
    for cut in shards[1:]:
        gain = gain * one(*cut)
    return gain


def routed_block(own_key, own, number, rows, number_of, top, reach, skew):
    sequence = jax.random.permutation(own_key, number_of)
    crowded, usual = portions_of(number_of, rows * top, reach, skew, True), portions_of(number_of, rows * top, reach, skew, False)
    places = jnp.arange(number_of)

    def named(tallies, turn):
        used = int((tallies > 0).sum())
        fixed = max(1, used // 4)
        shifted = fixed + (places - fixed + turn * (used - fixed)) % max(1, number_of - fixed)
        return jnp.zeros((number_of,), jnp.int32).at[sequence[jnp.where(places < fixed, places, shifted)]].set(jnp.asarray(tallies, jnp.int32))

    tallies = jnp.where(number % 4 == 0, named(crowded, number // 4), named(usual, number - number // 4 - 1))
    mixed = jax.random.permutation(jax.random.fold_in(own, 3), number_of)
    source_of, taker = mixed[0:number_of // 2 * 2:2], mixed[1:number_of // 2 * 2:2]
    margin = jnp.minimum(tallies[source_of] - 1, reach - tallies[taker]) // 2
    margin = jnp.where((source_of == sequence[0]) | (taker == sequence[0]) | (tallies[taker] == 0), 0, jnp.maximum(margin, 0))
    shifted = jax.random.randint(jax.random.fold_in(own, 4), (number_of // 2,), 0, 1 << 20) % (margin + 1)
    tallies = tallies.at[source_of].add(-shifted).at[taker].add(shifted)
    items = jnp.searchsorted(jnp.cumsum(tallies), jnp.arange(rows * top), side="right").astype(jnp.int32)
    grid = items.reshape(top, rows).T
    grid = grid[jax.random.permutation(jax.random.fold_in(own, 1), rows)]
    turn = jax.random.randint(jax.random.fold_in(own, 2), (rows, 1), 0, top)
    return jnp.take_along_axis(grid, (jnp.arange(top)[None, :] + turn) % top, axis=1)


def portions_of(number_of, total, most, lean, full):
    portions = [(1 << 20) // math.isqrt(rank ** lean) + 1 for rank in range(1, number_of + 1)]
    largest = most if full else min(most, max(-(-total // number_of), total * portions[0] // sum(portions)))
    least = 1 if total - largest >= number_of - 1 else 0
    given, surplus = [largest] + [least] * (number_of - 1), total - largest - least * (number_of - 1)
    while surplus > 0:
        free = [i for i in range(1, number_of) if given[i] < largest] or [i for i in range(1, number_of) if given[i] < most]
        mass, budget = sum([portions[i] for i in free]), surplus
        for i in free:
            extra = min(most - given[i], max(1, budget * portions[i] // mass), surplus)
            given[i] = given[i] + extra
            surplus = surplus - extra
    return np.array(given)


def scatter_about(own_key, dims, deviation, most, cuts=(), kind=jnp.bfloat16):
    gain = levels(own_key, dims, cuts, -0.22, 0.18) if cuts else 1.0
    result = jax.random.normal(own_key, dims, jnp.float32) * deviation * gain
    return jnp.minimum(jnp.maximum(result, -most), most).astype(kind)


def setup_inputs(seed: int = 0) -> dict:
    key_list = jax.random.split(jax.random.key(seed), 14)
    queries = draw_queries(jax.random.fold_in(key_list[13], 71), 0)
    cached_key_rows = scatter_about(key_list[1], (TOTAL_SEQUENCES * SHARING_DEVICES, CACHED_POSITIONS, KEY_VALUE_HEADS // SHARING_DEVICES * HEAD_SIZE), 1.0, 6.0, ((0, 1024),))
    cached_value_rows = scatter_about(key_list[2], (TOTAL_SEQUENCES * SHARING_DEVICES, CACHED_POSITIONS, KEY_VALUE_HEADS // SHARING_DEVICES * HEAD_SIZE), 1.0, 6.0, ((0, 1024),))
    incoming_keys = scatter_about(key_list[3], (TOTAL_SEQUENCES * SHARING_DEVICES, KEY_VALUE_HEADS // SHARING_DEVICES * HEAD_SIZE), 1.0, 6.0, ((0, 1024),))
    incoming_values = scatter_about(key_list[4], (TOTAL_SEQUENCES * SHARING_DEVICES, KEY_VALUE_HEADS // SHARING_DEVICES * HEAD_SIZE), 1.0, 6.0, ((0, 1024),))
    lengths = draw_lengths(jax.random.fold_in(key_list[13], 71), 0)
    residual = scatter_about(key_list[6], (TOTAL_SEQUENCES, D), 1.0, 6.0, ((0, 16),))
    norm_gain = jnp.clip(1.0 + 0.15 * jax.random.normal(key_list[7], (D,), jnp.float32), 0.25, 1.75)
    expert_ids_keys = jax.random.split(jax.random.fold_in(key_list[8], 1), TOTAL_SEQUENCES // TOK_GRP)
    expert_ids_turns = jax.random.permutation(jax.random.fold_in(key_list[8], 3), TOTAL_SEQUENCES // TOK_GRP)
    expert_ids = jax.vmap(lambda own, number: routed_block(jax.random.fold_in(key_list[8], 2), own, number, TOK_GRP, E, TOPK, ROWCAP, 2))(expert_ids_keys, expert_ids_turns).reshape((TOTAL_SEQUENCES, TOPK))
    route_logits = scatter_about(key_list[9], (TOTAL_SEQUENCES, TOPK), 1.5, 6.0, ((0, 16),), jnp.float32)
    w_gate = scatter_about(key_list[10], (D, E * FF), D ** -0.5, 0.078125, ((1, 1024),))
    w_up = scatter_about(key_list[11], (D, E * FF), D ** -0.5, 0.078125, ((1, 1024),))
    w_down = scatter_about(key_list[12], (E * FF, D), FF ** -0.5, 0.0625, ((0, 1024),))
    return {"queries": queries, "cached_key_rows": cached_key_rows, "cached_value_rows": cached_value_rows, "incoming_keys": incoming_keys, "incoming_values": incoming_values, "lengths": lengths, "residual": residual, "norm_gain": norm_gain, "expert_ids": expert_ids, "route_logits": route_logits, "w_gate": w_gate, "w_up": w_up, "w_down": w_down}


def slot_matrix(id_rows, prob_rows, expert, slot_cap):
    matched = (id_rows == expert).astype(jnp.int32).reshape(-1)
    position = (jnp.cumsum(matched) - matched).astype(jnp.int32)
    slot_hit = (position[None, :] == jnp.arange(slot_cap, dtype=jnp.int32)[:, None]) & (matched[None, :] > 0)
    slot_hit = slot_hit.astype(jnp.float32).reshape(slot_cap, id_rows.shape[0], id_rows.shape[1])
    return (lax.optimization_barrier(jnp.sum(slot_hit, axis=2)), lax.optimization_barrier(jnp.sum(slot_hit * prob_rows[None], axis=(1, 2))))

def attend_row(packed):
    query_vec, key_rows, value_rows, key_fresh, value_fresh, length_row = packed
    head_local = key_rows.shape[1] // HEAD_SIZE
    query_group_width = QUERY_HEADS // KEY_VALUE_HEADS
    score_scale = HEAD_SIZE ** (-0.5)
    query_mat = query_vec.astype(jnp.float32).reshape(head_local, query_group_width, HEAD_SIZE)
    key_mat = key_rows.astype(jnp.float32).reshape(CACHED_POSITIONS, head_local, HEAD_SIZE)
    value_mat = value_rows.astype(jnp.float32).reshape(CACHED_POSITIONS, head_local, HEAD_SIZE)
    score_all = jnp.einsum('hgd,thd->hgt', query_mat, key_mat) * score_scale
    mask_live = jnp.arange(CACHED_POSITIONS, dtype=jnp.int32) < length_row
    score_all = jnp.where(mask_live[None, None, :], score_all, -1e+30)
    new_score = jnp.einsum('hgd,hd->hg', query_mat, key_fresh.astype(jnp.float32).reshape(head_local, HEAD_SIZE)) * score_scale
    row_max = jnp.maximum(lax.optimization_barrier(jnp.max(score_all, axis=-1)), new_score)
    exp_all = jnp.exp(score_all - row_max[..., None])
    exp_new = jnp.exp(new_score - row_max)
    denom_all = lax.optimization_barrier(jnp.sum(exp_all, axis=-1)) + exp_new
    attn_weights = lax.optimization_barrier((exp_all / denom_all[..., None]).astype(jnp.bfloat16)).astype(jnp.float32)
    weight_new = lax.optimization_barrier((exp_new / denom_all).astype(jnp.bfloat16)).astype(jnp.float32)
    mixed_out = jnp.einsum('hgt,thd->hgd', attn_weights, value_mat)
    mixed_out = mixed_out + weight_new[..., None] * value_fresh.astype(jnp.float32).reshape(head_local, 1, HEAD_SIZE)
    return mixed_out.reshape(-1).astype(jnp.bfloat16)

def reference(queries, cached_key_rows, cached_value_rows, incoming_keys, incoming_values, lengths, residual, norm_gain, expert_ids, route_logits, w_gate, w_up, w_down):
    row_lengths = jnp.repeat(lengths, SHARING_DEVICES).astype(jnp.int32)
    attended = lax.map(attend_row, (queries, cached_key_rows, cached_value_rows, incoming_keys, incoming_values, row_lengths))
    heads_all = attended.reshape(TOTAL_SEQUENCES, D)
    summed = residual.astype(jnp.float32) + heads_all.astype(jnp.float32)
    normed = (summed * lax.rsqrt(lax.optimization_barrier(jnp.mean(summed * summed, axis=-1, keepdims=True)) + 1e-05) * norm_gain).astype(jnp.bfloat16)
    route_probs = jax.nn.softmax(route_logits.astype(jnp.float32), axis=-1)
    group_ids = expert_ids.reshape(N_GRP, TOK_GRP, TOPK)
    group_probs = route_probs.reshape(N_GRP, TOK_GRP, TOPK)
    group_rows = normed.astype(jnp.float32).reshape(N_GRP, TOK_GRP, D)
    total_out = jnp.zeros((N_GRP, TOK_GRP, D), jnp.float32)
    for expert in range(E):

        def one_group(id_rows, prob_rows):
            return slot_matrix(id_rows, prob_rows, expert, ROWCAP)
        select_all, slot_weight = jax.vmap(one_group)(group_ids, group_probs)
        picked = jnp.einsum('gct,gtd->gcd', select_all, group_rows).astype(jnp.bfloat16).reshape(N_GRP * ROWCAP, D)
        gate_out = jnp.dot(picked, w_gate[:, expert * FF:(expert + 1) * FF], preferred_element_type=jnp.float32)
        up_out = jnp.dot(picked, w_up[:, expert * FF:(expert + 1) * FF], preferred_element_type=jnp.float32)
        hidden = (jax.nn.silu(gate_out) * up_out).astype(jnp.bfloat16)
        expert_out = jnp.dot(hidden, w_down[expert * FF:(expert + 1) * FF], preferred_element_type=jnp.float32)
        expert_out = expert_out.reshape(N_GRP, ROWCAP, D)
        total_out = total_out + jnp.einsum('gct,gc,gcd->gtd', select_all, slot_weight, expert_out, precision=lax.Precision.HIGHEST)
    return total_out.reshape(TOTAL_SEQUENCES, D).astype(jnp.bfloat16)
```

```python
import jax
import jax.numpy as jnp
from jax import lax
from jax.experimental import pallas as pl
from jax.experimental.pallas import tpu as pltpu
from jax.sharding import PartitionSpec as P

BF = jnp.bfloat16
F32 = jnp.float32
I32 = jnp.int32
D = 6144
HALF = 3072
NG = 16
SLICE = 384
CAP = 10
ROWS = 160
MESH = pl.DeviceIdType.MESH


def iota(shape, dim):
    return lax.broadcasted_iota(I32, shape, dim)


def kernel(
    q_ref, kn_ref, vn_ref, len_ref, ids_ref, lg_ref,
    k_hbm, v_hbm, res_hbm, gain_hbm, wg_hbm, wu_hbm, wd_hbm,
    out_ref,
    k_v, v_v, res_v, gain_v,
    qs, res24, att24, sq_send, sq_recv, tok, wgu_r, wd_r,
    pk_send, pk_recv, rs_send, rs_recv, hid_send, hid_recv,
    lr_send, lr_recv, fin_send, fin_recv,
    loc_sem, sq_sem, a_ss, a_rs, l_ss, l_rs, wg_ss, wg_rs, wu_ss, wu_rs, wd_ss, wd_rs,
    pk_ss, pk_rs, rs_ss, rs_rs, hid_ss, hid_rs, lr_ss, lr_rs, fin_ss, fin_rs,
):
    g = lax.axis_index("grp")
    d = lax.axis_index("dev")
    a = d // 8
    part = d % 8
    b = part // 2
    c = d % 2

    def did(gg, dd):
        return (gg, dd)

    def rc(src, dst, ss, rs, dev):
        return pltpu.make_async_remote_copy(
            src_ref=src, dst_ref=dst, send_sem=ss, recv_sem=rs,
            device_id=dev, device_id_type=MESH,
        )

    barrier = pltpu.get_barrier_semaphore()

    def sig(dev):
        pl.semaphore_signal(barrier, inc=1, device_id=dev, device_id_type=MESH)

    def sig_far(k, x):
        sig(did(g, ((a + k) % 8) * 8 + part))
        return x

    def fin_out(k):
        return 2 * part + k // 4, 4 * g + k % 4

    def fin_in(e):
        return d // 4, e * 8 + g // 2

    def is_me(gg, dd):
        return jnp.logical_and(gg == g, dd == d)

    lax.fori_loop(1, 8, sig_far, 0)

    def sig_fin(k, x):
        go, do = fin_out(k)
        gi, di = fin_in(k)

        @pl.when(jnp.logical_not(is_me(go, do)))
        def _():
            sig(did(go, do))

        @pl.when(jnp.logical_not(is_me(gi, di)))
        def _():
            sig(did(gi, di))

        return x

    lax.fori_loop(0, 8, sig_fin, 0)
    d_other = d + 1 - 2 * c

    def sig_line(k, x):
        sig(did(g, a * 8 + ((b + k) % 4) * 2 + c))
        sig(did(g, a * 8 + ((b + k) % 4) * 2 + 1 - c))
        return x

    lax.fori_loop(1, 4, sig_line, 0)

    def sig_xy(k, x):
        sig(did((g + k) % NG, d))
        sig(did((g + k) % NG, d_other))
        return x

    lax.fori_loop(1, NG, sig_xy, 0)
    sig(did(g, d_other))

    half_at = pl.multiple_of(c * HALF, HALF)
    loads = [
        pltpu.make_async_copy(k_hbm, k_v, loc_sem.at[0]),
        pltpu.make_async_copy(v_hbm, v_v, loc_sem.at[1]),
        pltpu.make_async_copy(res_hbm.at[:, pl.ds(half_at, HALF)], res_v, loc_sem.at[2]),
        pltpu.make_async_copy(gain_hbm.at[pl.ds(pl.multiple_of(c * 24, 8), 24)], gain_v, loc_sem.at[3]),
    ]
    for cp in loads:
        cp.start()

    token = d // 2
    length = len_ref[token]
    qs[...] = jnp.zeros_like(qs)
    q_row = q_ref[...].astype(F32)
    for i in range(24):
        qs[8 * (i // 6) + i % 6 : 8 * (i // 6) + i % 6 + 1, :] = q_row[:, 128 * i : 128 * i + 128]
    kn = kn_ref[...].astype(F32)
    vn = vn_ref[...].astype(F32)
    live = iota((8, 512), 1) < length
    scale = 128 ** (-0.5)
    loads[0].wait()
    loads[1].wait()
    for h in range(4):
        cols = slice(128 * h, 128 * h + 128)
        q_h = qs[8 * h : 8 * h + 8, :]
        s = lax.dot_general(
            q_h.astype(BF), k_v[:, cols], (((1,), (1,)), ((), ())), preferred_element_type=F32
        ) * scale
        s = jnp.where(live, s, -1e30)
        s_new = jnp.sum(q_h * kn[:, cols], axis=1, keepdims=True) * scale
        top = jnp.maximum(jnp.max(s, axis=1, keepdims=True), s_new)
        e = jnp.exp(s - top)
        e_new = jnp.exp(s_new - top)
        den = jnp.sum(e, axis=1, keepdims=True) + e_new
        o = jnp.dot((e / den).astype(BF), v_v[:, cols], preferred_element_type=F32)
        o = o + (e_new / den).astype(BF).astype(F32) * vn[:, cols]
        att24[6 * h : 6 * h + 6, :] = o[0:6, :].astype(BF).astype(F32)
    loads[2].wait()
    mine = iota((32, HALF), 0) == token
    res_row = jnp.sum(jnp.where(mine, res_v[...].astype(F32), 0.0), axis=0, keepdims=True)
    for i in range(24):
        res24[i : i + 1, :] = res_row[:, 128 * i : 128 * i + 128]
    summed = att24[...] + res24[...]
    sq = jnp.sum(jnp.sum(summed * summed, axis=1, keepdims=True), axis=0, keepdims=True)
    sq_send[...] = jnp.broadcast_to(sq, (8, 128))

    me_out = jnp.logical_and(g // 2 == part, d // 4 == g)
    pl.semaphore_wait(barrier, 15 * 2 + 1 + 7 + 6 + 16 - 2 * me_out.astype(I32))

    sq_copy = rc(sq_send, sq_recv, sq_sem.at[0], sq_sem.at[1], did(g, d_other))
    sq_copy.start()

    ids = ids_ref[...]
    id0, id1 = ids[0:1, :], ids[1:2, :]
    lg = lg_ref[...]
    l0, l1 = lg[0:1, :], lg[1:2, :]
    lm = jnp.maximum(l0, l1)
    e0, e1 = jnp.exp(l0 - lm), jnp.exp(l1 - lm)
    p0, p1 = e0 / (e0 + e1), e1 / (e0 + e1)
    before = jnp.where(iota((32, 32), 0) < iota((32, 32), 1), 1.0, 0.0).astype(BF)
    own = jnp.where(id0 == a, 1.0, 0.0) + jnp.where(id1 == a, 1.0, 0.0)
    own = jnp.broadcast_to(own, (16, 32))
    own_pos = jnp.dot(own.astype(BF), before, preferred_element_type=F32)
    pick_hot = jnp.where(own_pos == iota((16, 32), 0).astype(F32), own, 0.0)
    at = iota((32, 1024), 1)
    spread = jnp.where(iota((32, 1024), 0) == ((at // 32) % 8) * 4 + at // 256, 1.0, 0.0)
    pick_exp = jnp.dot(pick_hot.astype(BF), spread.astype(BF), preferred_element_type=F32)
    in_tok = iota((16, 1024), 1) % 32
    select = jnp.concatenate(
        [jnp.where(in_tok == j, pick_exp, 0.0).astype(BF) for j in range(24)], axis=0
    )

    loads[3].wait()
    sq_copy.wait_recv()
    total = sq_send[...] + sq_recv[...]
    inv = lax.rsqrt(total[0:1, 0:1] * (1.0 / D) + 1e-05)
    normed = summed * inv * gain_v[...]
    tok[b, a] = jnp.concatenate([normed, jnp.zeros((8, 128), F32)], axis=0).astype(BF)

    def a_copy(k):
        aa = (a + k) % 8
        return rc(tok.at[b, a], tok.at[b, a], a_ss.at[k], a_rs.at[a], did(g, aa * 8 + part))

    def a_wait(k):
        aa = (a + k) % 8
        return rc(tok.at[b, aa], tok.at[b, aa], a_ss.at[k], a_rs.at[aa], did(g, aa * 8 + part))

    for k in (4, 3, 5, 2, 6, 1, 7):
        a_copy(k).start()

    def cut(ref, gg):
        return ref.at[:, pl.ds(pl.multiple_of(SLICE * gg, 128), SLICE)]

    def wg_copy(k, src_g, dst_g):
        return rc(cut(wg_hbm, dst_g), wgu_r.at[src_g, pl.ds(0, 64)], wg_ss.at[k], wg_rs.at[src_g], did(dst_g, d))

    def wu_copy(k, src_g, dst_g):
        return rc(cut(wu_hbm, dst_g), wgu_r.at[src_g, pl.ds(64, 64)], wu_ss.at[k], wu_rs.at[src_g], did(dst_g, d))

    def wd_copy(k, src_g, dst_g):
        return rc(
            cut(wd_hbm, dst_g), wd_r.at[src_g],
            wd_ss.at[k], wd_rs.at[src_g], did(dst_g, d))

    def reshard(k, x):
        wg_copy(k, g, (g + k) % NG).start()
        wu_copy(k, g, (g + k) % NG).start()
        return x

    def reshard_down(k, x):
        wd_copy(k, g, (g + k) % NG).start()
        return x

    lax.fori_loop(1, NG, reshard, 0)
    lax.fori_loop(1, NG, reshard_down, 0)
    wg_own = pltpu.make_async_copy(cut(wg_hbm, g), wgu_r.at[g, pl.ds(0, 64)], loc_sem.at[4])
    wu_own = pltpu.make_async_copy(cut(wu_hbm, g), wgu_r.at[g, pl.ds(64, 64)], loc_sem.at[5])
    wd_own = pltpu.make_async_copy(cut(wd_hbm, g), wd_r.at[g], loc_sem.at[6])
    wg_own.start()
    wu_own.start()
    wd_own.start()

    def a_arrive(k, x):
        a_wait(k).wait_recv()
        return x

    lax.fori_loop(1, 8, a_arrive, 0)

    def l_copy(k):
        return rc(tok.at[b], tok.at[b], l_ss.at[k], l_rs.at[b],
                  did(g, a * 8 + ((b + k) % 4) * 2 + c))

    def l_wait(k):
        bb = (b + k) % 4
        return rc(tok.at[bb], tok.at[bb], l_ss.at[k], l_rs.at[bb], did(g, a * 8 + bb * 2 + c))

    for k in (1, 2, 3):
        l_copy(k).start()
    for k in (1, 2, 3):
        l_wait(k).wait_recv()

    picked = jnp.dot(select, tok[...].reshape(1024, 128), preferred_element_type=F32).astype(BF)
    for k in range(8):
        pk_send[k] = picked[48 * k : 48 * k + 48, :]

    def pk_out(k, x):
        gg = 8 * c + (g + k // 2) % 8
        dd = a * 8 + b * 2 + (c + k) % 2
        cp = rc(pk_send.at[(g + k // 2) % 8], pk_recv.at[g], pk_ss.at[k], pk_rs.at[g], did(gg, dd))

        @pl.when(jnp.logical_not(is_me(gg, dd)))
        def _():
            cp.start()

        @pl.when(is_me(gg, dd))
        def _():
            pk_recv[g] = pk_send[(g + k // 2) % 8]

        return x

    lax.fori_loop(0, 16, pk_out, 0)

    pk_from = a * 8 + b * 2 + g // 8

    def pk_in(k, x):
        gg = (g + k) % NG

        @pl.when(jnp.logical_not(is_me(gg, pk_from)))
        def _():
            rc(pk_send.at[0], pk_recv.at[gg], pk_ss.at[k], pk_rs.at[gg], did(gg, pk_from)).wait_recv()

        return x

    lax.fori_loop(0, NG, pk_in, 0)
    squeeze = jnp.where(
        iota((ROWS, 256), 1) == (iota((ROWS, 256), 0) // CAP) * 16 + iota((ROWS, 256), 0) % CAP, 1.0, 0.0
    ).astype(BF)
    x_rows = jnp.concatenate(
        [
            jnp.dot(
                squeeze, pk_recv[:, 16 * j : 16 * j + 16, :].reshape(256, 128),
                preferred_element_type=F32,
            ).astype(BF)
            for j in range(3)
        ],
        axis=1,
    )

    def gu_in(k, x):
        gg = (g + k) % NG
        wg_copy(k, gg, g).wait_recv()
        wu_copy(k, gg, g).wait_recv()
        return x

    wg_own.wait()
    wu_own.wait()
    lax.fori_loop(1, NG, gu_in, 0)

    def rs_copy(src_g, dst_g):
        return rc(rs_send.at[dst_g], rs_recv.at[src_g], rs_ss.at[dst_g], rs_rs.at[src_g], did(dst_g, d))

    def rs_out(i, x):
        chunk = (g // 4 + i) % 4
        y = lax.dot_general(
            x_rows, wgu_r[pl.ds(4 * chunk, 4)].reshape(512, SLICE), (((1,), (1,)), ((), ())),
            preferred_element_type=F32,
        ).astype(BF)
        for j in range(4):
            rs_send[4 * chunk + j] = y[:, 128 * j : 128 * j + 128]
        for j in range(4):
            gg = 4 * chunk + j

            @pl.when(gg != g)
            def _():
                rs_copy(g, gg).start()

        return x

    lax.fori_loop(0, 4, rs_out, 0)
    rs_recv[g] = rs_send[g]

    def rs_in(k, x):
        rs_copy((g + k) % NG, g).wait_recv()
        return x

    lax.fori_loop(1, NG, rs_in, 0)
    both = jnp.sum(rs_recv[...].astype(F32), axis=0)
    gate, up = both[:, :64], both[:, 64:]
    hidden = (gate / (1.0 + jnp.exp(-gate)) * up)
    hid_send[...] = jnp.concatenate([hidden[:80], hidden[80:]], axis=1).astype(BF)
    hid_recv[g] = hid_send[...]

    def hid_copy(k, src_g, dst_g):
        return rc(hid_send, hid_recv.at[src_g], hid_ss.at[k], hid_rs.at[src_g], did(dst_g, d))

    def hid_out(k, x):
        hid_copy(k, g, (g + k) % NG).start()
        return x

    lax.fori_loop(1, NG, hid_out, 0)
    wd_own.wait()

    def wd_in(k, x):
        wd_copy(k, (g + k) % NG, g).wait_recv()
        return x

    lax.fori_loop(1, NG, wd_in, 0)

    def hid_in(k, x):
        hid_copy(k, (g + k) % NG, g).wait_recv()
        return x

    lax.fori_loop(1, NG, hid_in, 0)
    tops, lows = [], []
    for i in range(8):
        h0, h1 = hid_recv[2 * i], hid_recv[2 * i + 1]
        tops.append(jnp.concatenate([h0[:, :64], h1[:, :64]], axis=1))
        lows.append(jnp.concatenate([h0[:, 64:], h1[:, 64:]], axis=1))
    hid_all = jnp.concatenate(
        [jnp.concatenate(tops, axis=1), jnp.concatenate(lows, axis=1)], axis=0
    )
    down = jnp.dot(hid_all, wd_r[...].reshape(1024, SLICE), preferred_element_type=F32).astype(BF)
    widen = jnp.where(
        jnp.logical_and(
            iota((256, ROWS), 1) == (iota((256, ROWS), 0) // 16) * CAP + iota((256, ROWS), 0) % 16,
            iota((256, ROWS), 0) % 16 < CAP,
        ), 1.0, 0.0,
    ).astype(BF)
    lr_send[...] = jnp.dot(widen, down, preferred_element_type=F32).astype(BF).reshape(8, 32, SLICE)

    def lr_copy(k, src_p, dst_p, dev_p):
        return rc(lr_send.at[dst_p], lr_recv.at[src_p], lr_ss.at[k], lr_rs.at[src_p],
                  did(g, a * 8 + dev_p))

    for k in range(1, 8):
        lr_copy(k, part, (part + k) % 8, (part + k) % 8).start()
    lr_recv[part] = lr_send[part]
    for k in range(1, 8):
        pp = (part + k) % 8
        lr_copy(k, pp, part, pp).wait_recv()
    rows = jnp.sum(lr_recv[...].astype(F32), axis=0)
    for k in range(8):
        piece = rows[16 * (k // 4) : 16 * (k // 4) + 16, 96 * (k % 4) : 96 * (k % 4) + 96]
        fin_send[k] = jnp.concatenate([piece, jnp.zeros((16, 32), F32)], axis=1).astype(BF)

    def fin_go(k, x):
        go, do = fin_out(k)

        @pl.when(jnp.logical_not(is_me(go, do)))
        def _():
            rc(fin_send.at[k], fin_recv.at[a], fin_ss.at[k], fin_rs.at[a], did(go, do)).start()

        @pl.when(is_me(go, do))
        def _():
            fin_recv[a] = fin_send[k]

        return x

    lax.fori_loop(0, 8, fin_go, 0)

    slot = iota((128, 32), 0)
    hit0 = jnp.where(id0 == slot // 16, 1.0, 0.0)
    hit1 = jnp.where(id1 == slot // 16, 1.0, 0.0)
    hits = hit0 + hit1
    places = jnp.dot(hits.astype(BF), before, preferred_element_type=F32)
    combine = jnp.where(places == (slot % 16).astype(F32), hit0 * p0 + hit1 * p1, 0.0)

    def fin_come(e, x):
        gi, di = fin_in(e)

        @pl.when(jnp.logical_not(is_me(gi, di)))
        def _():
            rc(fin_send.at[0], fin_recv.at[e], fin_ss.at[e], fin_rs.at[e], did(gi, di)).wait_recv()

        return x

    lax.fori_loop(0, 8, fin_come, 0)
    result = lax.dot_general(
        combine, fin_recv[...].reshape(128, 128).astype(F32), (((0,), (0,)), ((), ())), precision=lax.Precision.HIGHEST,
        preferred_element_type=F32,
    )
    out_ref[...] = result[:, :96].astype(BF)

    sq_copy.wait_send()

    def a_left(k, x):
        a_copy(k).wait_send()
        return x

    lax.fori_loop(1, 8, a_left, 0)
    for k in (1, 2, 3):
        l_copy(k).wait_send()

    def xy_left(k, x):
        gg = (g + k) % NG
        wg_copy(k, g, gg).wait_send()
        wu_copy(k, g, gg).wait_send()
        wd_copy(k, g, gg).wait_send()
        rs_copy(g, gg).wait_send()
        hid_copy(k, g, gg).wait_send()
        return x

    lax.fori_loop(1, NG, xy_left, 0)

    def pk_left(k, x):
        gg = 8 * c + (g + k // 2) % 8
        dd = a * 8 + b * 2 + (c + k) % 2

        @pl.when(jnp.logical_not(is_me(gg, dd)))
        def _():
            rc(pk_send.at[(g + k // 2) % 8], pk_recv.at[g], pk_ss.at[k], pk_rs.at[g], did(gg, dd)).wait_send()

        return x

    lax.fori_loop(0, 16, pk_left, 0)
    for k in range(1, 8):
        lr_copy(k, part, (part + k) % 8, (part + k) % 8).wait_send()

    def fin_left(k, x):
        go, do = fin_out(k)

        @pl.when(jnp.logical_not(is_me(go, do)))
        def _():
            rc(fin_send.at[k], fin_recv.at[a], fin_ss.at[k], fin_rs.at[a], did(go, do)).wait_send()

        return x

    lax.fori_loop(0, 8, fin_left, 0)


def body(
    queries, cached_key_rows, cached_value_rows, incoming_keys, incoming_values, lengths,
    residual, norm_gain, expert_ids, route_logits, w_gate, w_up, w_down,
):
    vmem = pl.BlockSpec(memory_space=pltpu.VMEM)
    anyw = pl.BlockSpec(memory_space=pl.ANY)
    dma = pltpu.SemaphoreType.DMA
    return pl.pallas_call(
        kernel,
        out_shape=jax.ShapeDtypeStruct((32, 96), BF),
        in_specs=[vmem, vmem, vmem, pl.BlockSpec(memory_space=pltpu.SMEM), vmem, vmem] + [anyw] * 7,
        out_specs=vmem,
        scratch_shapes=[
            pltpu.VMEM((512, 512), BF),
            pltpu.VMEM((512, 512), BF),
            pltpu.VMEM((32, HALF), BF),
            pltpu.VMEM((24, 128), F32),
            pltpu.VMEM((32, 128), F32),
            pltpu.VMEM((24, 128), F32),
            pltpu.VMEM((24, 128), F32),
            pltpu.VMEM((8, 128), F32),
            pltpu.VMEM((8, 128), F32),
            pltpu.VMEM((4, 8, 32, 128), BF),
            pltpu.VMEM((NG, 128, SLICE), BF),
            pltpu.VMEM((NG, 64, SLICE), BF),
            pltpu.VMEM((8, 48, 128), BF),
            pltpu.VMEM((NG, 48, 128), BF),
            pltpu.VMEM((NG, ROWS, 128), BF),
            pltpu.VMEM((NG, ROWS, 128), BF),
            pltpu.VMEM((80, 128), BF),
            pltpu.VMEM((NG, 80, 128), BF),
            pltpu.VMEM((8, 32, SLICE), BF),
            pltpu.VMEM((8, 32, SLICE), BF),
            pltpu.VMEM((8, 16, 128), BF),
            pltpu.VMEM((8, 16, 128), BF),
            dma((7,)), dma((2,)), dma((8,)), dma((8,)), dma((4,)), dma((4,)),
            dma((NG,)), dma((NG,)), dma((NG,)), dma((NG,)), dma((NG,)), dma((NG,)),
            dma((NG,)), dma((NG,)), dma((NG,)), dma((NG,)), dma((NG,)), dma((NG,)),
            dma((8,)), dma((8,)), dma((8,)), dma((8,)),
        ],
        compiler_params=pltpu.CompilerParams(
            collective_id=0, has_side_effects=True, vmem_limit_bytes=67000000
        ),
    )(
        queries, incoming_keys, incoming_values, lengths, expert_ids.T, route_logits.T,
        cached_key_rows.reshape(512, 512), cached_value_rows.reshape(512, 512), residual,
        norm_gain.reshape(48, 128), w_gate.T, w_up.T, w_down,
    )


def solution(mesh):
    return jax.shard_map(
        body,
        mesh=mesh,
        in_specs=(
            P(("grp", "dev"), None),
            P(("grp", "dev"), None, None),
            P(("grp", "dev"), None, None),
            P(("grp", "dev"), None),
            P(("grp", "dev"), None),
            P("grp"),
            P("grp", None),
            P(),
            P("grp", None),
            P("grp", None),
            P(None, ("dev", "grp")),
            P(None, ("dev", "grp")),
            P(("dev", "grp"), None),
        ),
        out_specs=P("grp", "dev"),
        check_vma=False,
    )
```

```python
import jax
import jax.numpy as jnp
from jax import lax
from jax.experimental import pallas as pl
from jax.experimental.pallas import tpu as pltpu
from jax.sharding import PartitionSpec as P

BF = jnp.bfloat16
F32 = jnp.float32
I32 = jnp.int32
D = 6144
HALF = 3072
NG = 16
SLICE = 384
CAP = 10
ROWS = 160
MESH = pl.DeviceIdType.MESH


def iota(shape, dim):
    return lax.broadcasted_iota(I32, shape, dim)


def kernel(
    q_hbm, kn_hbm, vn_hbm, len_hbm, ids_hbm, lg_hbm,
    k_hbm, v_hbm, res_hbm, gain_hbm, wg_hbm, wu_hbm, wd_hbm,
    out_ref,
    q_ref, kn_ref, vn_ref, len_ref, ids_ref, lg_ref,
    k_v, v_v, res_v, gain_v,
    qs, res24, att24, sq_send, sq_recv, tok, wk, wd_r,
    agb, gu_send, gu_recv, hid_send, hid_recv,
    lr_send, lr_recv, fin_send, fin_recv,
    loc_sem, sq_sem, a_ss, a_rs, l_ss, l_rs, wk_ss, wk_rs, wd_ss, wd_rs,
    ag_ss, ag_rs, gu_sem, hid_ss, hid_rs, lr_ss, lr_rs, fin_ss, fin_rs,
):
    g = lax.axis_index("grp")
    d = lax.axis_index("dev")
    a = d // 8
    part = d % 8
    b = part // 2
    c = d % 2
    xg = g // 4
    yg = g % 4

    def did(gg, dd):
        return (gg, dd)

    def rc(src, dst, ss, rs, dev):
        return pltpu.make_async_remote_copy(
            src_ref=src, dst_ref=dst, send_sem=ss, recv_sem=rs,
            device_id=dev, device_id_type=MESH,
        )

    barrier = pltpu.get_barrier_semaphore()

    def sig(dev):
        pl.semaphore_signal(barrier, inc=1, device_id=dev, device_id_type=MESH)

    def sig_far(k, x):
        sig(did(g, ((a + k) % 8) * 8 + part))
        return x

    def fin_out(k):
        return 2 * part + k // 4, 4 * g + k % 4

    def fin_in(e):
        return d // 4, e * 8 + g // 2

    def is_me(gg, dd):
        return jnp.logical_and(gg == g, dd == d)

    lax.fori_loop(1, 8, sig_far, 0)

    d_other = d + 1 - 2 * c

    def sig_line(k, x):
        sig(did(g, a * 8 + ((b + k) % 4) * 2 + c))
        return x

    lax.fori_loop(1, 4, sig_line, 0)

    def sig_xy(k, x):
        sig(did((g + k) % NG, d))
        return x

    lax.fori_loop(1, NG, sig_xy, 0)
    sig(did(g, d_other))

    half_at = pl.multiple_of(c * HALF, HALF)
    loads = [
        pltpu.make_async_copy(k_hbm, k_v, loc_sem.at[0]),
        pltpu.make_async_copy(v_hbm, v_v, loc_sem.at[1]),
        pltpu.make_async_copy(res_hbm.at[:, pl.ds(half_at, HALF)], res_v, loc_sem.at[2]),
        pltpu.make_async_copy(gain_hbm.at[pl.ds(pl.multiple_of(c * 24, 8), 24)], gain_v, loc_sem.at[3]),
    ]
    small = [
        pltpu.make_async_copy(src, dst, loc_sem.at[7 + i])
        for i, (src, dst) in enumerate([
            (q_hbm, q_ref), (len_hbm, len_ref), (kn_hbm, kn_ref), (vn_hbm, vn_ref),
            (ids_hbm, ids_ref), (lg_hbm, lg_ref)])
    ]
    for cp in small + loads:
        cp.start()

    token = d // 2
    for cp in small:
        cp.wait()
    length = len_ref[token]
    qs[...] = jnp.zeros_like(qs)
    q_row = q_ref[...].astype(F32)
    for i in range(24):
        qs[8 * (i // 6) + i % 6 : 8 * (i // 6) + i % 6 + 1, :] = q_row[:, 128 * i : 128 * i + 128]
    kn = kn_ref[...].astype(F32)
    vn = vn_ref[...].astype(F32)
    live = iota((8, 512), 1) < length
    scale = 128 ** (-0.5)
    loads[0].wait()
    loads[1].wait()
    for h in range(4):
        cols = slice(128 * h, 128 * h + 128)
        q_h = qs[8 * h : 8 * h + 8, :]
        s = lax.dot_general(
            q_h.astype(BF), k_v[:, cols], (((1,), (1,)), ((), ())), preferred_element_type=F32
        ) * scale
        s = jnp.where(live, s, -1e30)
        s_new = jnp.sum(q_h * kn[:, cols], axis=1, keepdims=True) * scale
        top = jnp.maximum(jnp.max(s, axis=1, keepdims=True), s_new)
        e = jnp.exp(s - top)
        e_new = jnp.exp(s_new - top)
        den = jnp.sum(e, axis=1, keepdims=True) + e_new
        o = jnp.dot((e / den).astype(BF), v_v[:, cols], preferred_element_type=F32)
        o = o + (e_new / den).astype(BF).astype(F32) * vn[:, cols]
        att24[6 * h : 6 * h + 6, :] = o[0:6, :].astype(BF).astype(F32)
    loads[2].wait()
    mine = iota((32, HALF), 0) == token
    res_row = jnp.sum(jnp.where(mine, res_v[...].astype(F32), 0.0), axis=0, keepdims=True)
    for i in range(24):
        res24[i : i + 1, :] = res_row[:, 128 * i : 128 * i + 128]
    summed = att24[...] + res24[...]
    sq = jnp.sum(jnp.sum(summed * summed, axis=1, keepdims=True), axis=0, keepdims=True)
    sq_send[...] = jnp.broadcast_to(sq, (8, 128))

    pl.semaphore_wait(barrier, 15 + 1 + 7 + 3)

    sq_copy = rc(sq_send, sq_recv, sq_sem.at[0], sq_sem.at[1], did(g, d_other))
    sq_copy.start()

    ids = ids_ref[...]
    id0, id1 = ids[0:1, :], ids[1:2, :]
    lg = lg_ref[...]
    l0, l1 = lg[0:1, :], lg[1:2, :]
    lm = jnp.maximum(l0, l1)
    e0, e1 = jnp.exp(l0 - lm), jnp.exp(l1 - lm)
    p0, p1 = e0 / (e0 + e1), e1 / (e0 + e1)
    before = jnp.where(iota((32, 32), 0) < iota((32, 32), 1), 1.0, 0.0).astype(BF)
    own = jnp.where(id0 == a, 1.0, 0.0) + jnp.where(id1 == a, 1.0, 0.0)
    own = jnp.broadcast_to(own, (16, 32))
    own_pos = jnp.dot(own.astype(BF), before, preferred_element_type=F32)
    pick_hot = jnp.where(own_pos == iota((16, 32), 0).astype(F32), own, 0.0)
    at = iota((32, 1024), 1)
    spread = jnp.where(iota((32, 1024), 0) == ((at // 32) % 8) * 4 + at // 256, 1.0, 0.0)
    pick_exp = jnp.dot(pick_hot.astype(BF), spread.astype(BF), preferred_element_type=F32)
    in_tok = iota((16, 1024), 1) % 32
    select = jnp.concatenate(
        [jnp.where(in_tok == j, pick_exp, 0.0).astype(BF) for j in range(24)], axis=0
    )

    loads[3].wait()
    sq_copy.wait_recv()
    total = sq_send[...] + sq_recv[...]
    inv = lax.rsqrt(total[0:1, 0:1] * (1.0 / D) + 1e-05)
    normed = summed * inv * gain_v[...]
    tok[b, a] = jnp.concatenate([normed, jnp.zeros((8, 128), F32)], axis=0).astype(BF)

    def a_copy(k):
        aa = (a + k) % 8
        return rc(tok.at[b, a], tok.at[b, a], a_ss.at[k], a_rs.at[a], did(g, aa * 8 + part))

    def a_wait(k):
        aa = (a + k) % 8
        return rc(tok.at[b, aa], tok.at[b, aa], a_ss.at[k], a_rs.at[aa], did(g, aa * 8 + part))

    for k in (4, 3, 5, 2, 6, 1, 7):
        a_copy(k).start()

    def cut(ref, gg):
        return ref.at[:, pl.ds(pl.multiple_of(SLICE * gg, 128), SLICE)]

    mine_half = pl.ds(half_at, HALF)
    other_half = pl.ds(pl.multiple_of((1 - c) * HALF, HALF), HALF)
    wk_copies = [
        rc(ref.at[:, other_half], wk.at[2 + i], wk_ss.at[i], wk_rs.at[i], did(g, d_other))
        for i, ref in enumerate((wg_hbm, wu_hbm))
    ]
    wk_own = [
        pltpu.make_async_copy(ref.at[:, mine_half], wk.at[i], loc_sem.at[4 + i])
        for i, ref in enumerate((wg_hbm, wu_hbm))
    ]

    def wd_copy(k, src_g, dst_g):
        return rc(
            cut(wd_hbm, dst_g), wd_r.at[src_g],
            wd_ss.at[k], wd_rs.at[src_g], did(dst_g, d))

    def reshard_down(k, x):
        wd_copy(k, g, (g + k) % NG).start()
        return x

    for cp in wk_copies + wk_own:
        cp.start()
    lax.fori_loop(1, NG, reshard_down, 0)
    wd_own = pltpu.make_async_copy(cut(wd_hbm, g), wd_r.at[g], loc_sem.at[6])
    wd_own.start()

    def a_arrive(k, x):
        a_wait(k).wait_recv()
        return x

    lax.fori_loop(1, 8, a_arrive, 0)

    def l_copy(k):
        return rc(tok.at[b], tok.at[b], l_ss.at[k], l_rs.at[b],
                  did(g, a * 8 + ((b + k) % 4) * 2 + c))

    def l_wait(k):
        bb = (b + k) % 4
        return rc(tok.at[bb], tok.at[bb], l_ss.at[k], l_rs.at[bb], did(g, a * 8 + bb * 2 + c))

    for k in (1, 2, 3):
        l_copy(k).start()
    for k in (1, 2, 3):
        l_wait(k).wait_recv()

    picked = jnp.dot(select, tok[...].reshape(1024, 128), preferred_element_type=F32).astype(BF)
    agb[xg, yg] = picked.reshape(24, 16, 128)

    def side(p, du, dv):
        dx, dy = (du, dv) if p == 0 else (dv, du)
        return did(((xg + dx + 4) % 4) * 4 + (yg + dy + 4) % 4, d)

    def ring(p, stage, off, j, n):
        u, v = (xg, yg) if p == 0 else (yg, xg)
        js = pl.ds(12 * p + j, n)
        if stage == 0:
            u = (u + off + 4) % 4
            return agb.at[u, v, js] if p == 0 else agb.at[v, u, js]
        v = (v + off + 4) % 4
        return agb.at[:, v, js] if p == 0 else agb.at[v, :, js]

    def hop(p, stage, off, j, n, way, number):
        piece = ring(p, stage, off, j, n)
        dev = side(p, way, 0) if stage == 0 else side(p, 0, way)
        at_sem = 4 * stage + number
        return rc(piece, piece, ag_ss.at[p, at_sem], ag_rs.at[p, at_sem], dev)

    left_ways = []
    for stage in range(2):
        for p in range(2):
            for way, number in ((1, 0), (-1, 1)):
                cp = hop(p, stage, 0, 0, 12, way, number)
                cp.start()
                left_ways.append(cp)
        for p in range(2):
            hop(p, stage, -1, 0, 12, 1, 0).wait_recv()
            cp = hop(p, stage, -1, 0, 6, 1, 2)
            cp.start()
            left_ways.append(cp)
            hop(p, stage, 1, 0, 12, -1, 1).wait_recv()
            cp = hop(p, stage, 1, 6, 6, -1, 3)
            cp.start()
            left_ways.append(cp)
        for p in range(2):
            hop(p, stage, -2, 0, 6, 1, 2).wait_recv()
            hop(p, stage, 2, 6, 6, -1, 3).wait_recv()

    for cp in wk_own:
        cp.wait()
    for cp in wk_copies:
        cp.wait_recv()
    x_rows = jnp.concatenate([agb[:, :, j].reshape(256, 128) for j in range(24)], axis=1)
    y = lax.dot_general(
        x_rows, wk[...].reshape(256, HALF), (((1,), (1,)), ((), ())), preferred_element_type=F32
    )
    gu_send[...] = y[:, 128:]
    gu_copy = rc(gu_send, gu_recv, gu_sem.at[0], gu_sem.at[1], did(g, d_other))
    gu_copy.start()
    squeeze = jnp.where(
        iota((ROWS, 256), 1) == (iota((ROWS, 256), 0) // CAP) * 16 + iota((ROWS, 256), 0) % CAP, 1.0, 0.0
    ).astype(BF)
    gu_copy.wait_recv()
    both = y[:, :128] + gu_recv[...]
    gate, up = both[:, :64], both[:, 64:]
    hidden = (gate / (1.0 + jnp.exp(-gate)) * up).astype(BF)
    hidden = jnp.dot(squeeze, hidden, preferred_element_type=F32)
    hid_send[...] = jnp.concatenate([hidden[:80], hidden[80:]], axis=1).astype(BF)
    hid_recv[g] = hid_send[...]

    def hid_copy(k, src_g, dst_g):
        return rc(hid_send, hid_recv.at[src_g], hid_ss.at[k], hid_rs.at[src_g], did(dst_g, d))

    def hid_out(k, x):
        hid_copy(k, g, (g + k) % NG).start()
        return x

    lax.fori_loop(1, NG, hid_out, 0)
    wd_own.wait()

    def wd_in(k, x):
        wd_copy(k, (g + k) % NG, g).wait_recv()
        return x

    lax.fori_loop(1, NG, wd_in, 0)

    def hid_in(k, x):
        hid_copy(k, (g + k) % NG, g).wait_recv()
        return x

    lax.fori_loop(1, NG, hid_in, 0)
    tops, lows = [], []
    for i in range(8):
        h0, h1 = hid_recv[2 * i], hid_recv[2 * i + 1]
        tops.append(jnp.concatenate([h0[:, :64], h1[:, :64]], axis=1))
        lows.append(jnp.concatenate([h0[:, 64:], h1[:, 64:]], axis=1))
    hid_all = jnp.concatenate(
        [jnp.concatenate(tops, axis=1), jnp.concatenate(lows, axis=1)], axis=0
    )
    down = jnp.dot(hid_all, wd_r[...].reshape(1024, SLICE), preferred_element_type=F32).astype(BF)
    widen = jnp.where(
        jnp.logical_and(
            iota((256, ROWS), 1) == (iota((256, ROWS), 0) // 16) * CAP + iota((256, ROWS), 0) % 16,
            iota((256, ROWS), 0) % 16 < CAP,
        ), 1.0, 0.0,
    ).astype(BF)
    lr_send[...] = jnp.dot(widen, down, preferred_element_type=F32).astype(BF).reshape(8, 32, SLICE)

    def lr_copy(k, src_p, dst_p, dev_p):
        return rc(lr_send.at[dst_p], lr_recv.at[src_p], lr_ss.at[k], lr_rs.at[src_p],
                  did(g, a * 8 + dev_p))

    for k in range(1, 8):
        lr_copy(k, part, (part + k) % 8, (part + k) % 8).start()
    lr_recv[part] = lr_send[part]
    for k in range(1, 8):
        pp = (part + k) % 8
        lr_copy(k, pp, part, pp).wait_recv()
    rows = jnp.sum(lr_recv[...].astype(F32), axis=0)
    for k in range(8):
        piece = rows[16 * (k // 4) : 16 * (k // 4) + 16, 96 * (k % 4) : 96 * (k % 4) + 96]
        fin_send[k] = jnp.concatenate([piece, jnp.zeros((16, 32), F32)], axis=1).astype(BF)

    def fin_go(k, x):
        go, do = fin_out(k)

        @pl.when(jnp.logical_not(is_me(go, do)))
        def _():
            rc(fin_send.at[k], fin_recv.at[a], fin_ss.at[k], fin_rs.at[a], did(go, do)).start()

        @pl.when(is_me(go, do))
        def _():
            fin_recv[a] = fin_send[k]

        return x

    lax.fori_loop(0, 8, fin_go, 0)

    slot = iota((128, 32), 0)
    hit0 = jnp.where(id0 == slot // 16, 1.0, 0.0)
    hit1 = jnp.where(id1 == slot // 16, 1.0, 0.0)
    hits = hit0 + hit1
    places = jnp.dot(hits.astype(BF), before, preferred_element_type=F32)
    combine = jnp.where(places == (slot % 16).astype(F32), hit0 * p0 + hit1 * p1, 0.0)

    def fin_come(e, x):
        gi, di = fin_in(e)

        @pl.when(jnp.logical_not(is_me(gi, di)))
        def _():
            rc(fin_send.at[0], fin_recv.at[e], fin_ss.at[e], fin_rs.at[e], did(gi, di)).wait_recv()

        return x

    lax.fori_loop(0, 8, fin_come, 0)
    result = lax.dot_general(
        combine, fin_recv[...].reshape(128, 128).astype(F32), (((0,), (0,)), ((), ())), precision=lax.Precision.HIGHEST,
        preferred_element_type=F32,
    )
    out_ref[...] = result[:, :96].astype(BF)

    sq_copy.wait_send()

    def a_left(k, x):
        a_copy(k).wait_send()
        return x

    lax.fori_loop(1, 8, a_left, 0)
    for k in (1, 2, 3):
        l_copy(k).wait_send()

    def xy_left(k, x):
        gg = (g + k) % NG
        wd_copy(k, g, gg).wait_send()
        hid_copy(k, g, gg).wait_send()
        return x

    lax.fori_loop(1, NG, xy_left, 0)

    for cp in left_ways + wk_copies + [gu_copy]:
        cp.wait_send()
    for k in range(1, 8):
        lr_copy(k, part, (part + k) % 8, (part + k) % 8).wait_send()

    def fin_left(k, x):
        go, do = fin_out(k)

        @pl.when(jnp.logical_not(is_me(go, do)))
        def _():
            rc(fin_send.at[k], fin_recv.at[a], fin_ss.at[k], fin_rs.at[a], did(go, do)).wait_send()

        return x

    lax.fori_loop(0, 8, fin_left, 0)


def body(
    queries, cached_key_rows, cached_value_rows, incoming_keys, incoming_values, lengths,
    residual, norm_gain, expert_ids, route_logits, w_gate, w_up, w_down,
):
    vmem = pl.BlockSpec(memory_space=pltpu.VMEM)
    anyw = pl.BlockSpec(memory_space=pl.ANY)
    dma = pltpu.SemaphoreType.DMA
    return pl.pallas_call(
        kernel,
        out_shape=jax.ShapeDtypeStruct((32, 96), BF),
        in_specs=[anyw] * 13,
        out_specs=vmem,
        scratch_shapes=[
            pltpu.VMEM((1, HALF), BF),
            pltpu.VMEM((1, 512), BF),
            pltpu.VMEM((1, 512), BF),
            pltpu.SMEM((32,), I32),
            pltpu.VMEM((2, 32), I32),
            pltpu.VMEM((2, 32), F32),
            pltpu.VMEM((512, 512), BF),
            pltpu.VMEM((512, 512), BF),
            pltpu.VMEM((32, HALF), BF),
            pltpu.VMEM((24, 128), F32),
            pltpu.VMEM((32, 128), F32),
            pltpu.VMEM((24, 128), F32),
            pltpu.VMEM((24, 128), F32),
            pltpu.VMEM((8, 128), F32),
            pltpu.VMEM((8, 128), F32),
            pltpu.VMEM((4, 8, 32, 128), BF),
            pltpu.VMEM((4, 64, HALF), BF),
            pltpu.VMEM((NG, 64, SLICE), BF),
            pltpu.VMEM((4, 4, 24, 16, 128), BF),
            pltpu.VMEM((256, 128), F32),
            pltpu.VMEM((256, 128), F32),
            pltpu.VMEM((80, 128), BF),
            pltpu.VMEM((NG, 80, 128), BF),
            pltpu.VMEM((8, 32, SLICE), BF),
            pltpu.VMEM((8, 32, SLICE), BF),
            pltpu.VMEM((8, 16, 128), BF),
            pltpu.VMEM((8, 16, 128), BF),
            dma((13,)), dma((2,)), dma((8,)), dma((8,)), dma((4,)), dma((4,)),
            dma((2,)), dma((2,)), dma((NG,)), dma((NG,)),
            dma((2, 8)), dma((2, 8)), dma((2,)), dma((NG,)), dma((NG,)),
            dma((8,)), dma((8,)), dma((8,)), dma((8,)),
        ],
        compiler_params=pltpu.CompilerParams(
            collective_id=0, has_side_effects=True, vmem_limit_bytes=67000000
        ),
    )(
        queries, incoming_keys, incoming_values, lengths, expert_ids.T, route_logits.T,
        cached_key_rows.reshape(512, 512), cached_value_rows.reshape(512, 512), residual,
        norm_gain.reshape(48, 128), w_gate.T, w_up.T, w_down,
    )


def solution(mesh):
    return jax.shard_map(
        body,
        mesh=mesh,
        in_specs=(
            P(("grp", "dev"), None),
            P(("grp", "dev"), None, None),
            P(("grp", "dev"), None, None),
            P(("grp", "dev"), None),
            P(("grp", "dev"), None),
            P("grp"),
            P("grp", None),
            P(),
            P("grp", None),
            P("grp", None),
            P(None, ("dev", "grp")),
            P(None, ("dev", "grp")),
            P(("dev", "grp"), None),
        ),
        out_specs=P("grp", "dev"),
        check_vma=False,
    )
```

```python
import jax
import jax.numpy as jnp
from jax import lax
from jax.experimental import pallas as pl
from jax.experimental.pallas import tpu as pltpu
from jax.sharding import PartitionSpec as P

BF = jnp.bfloat16
F32 = jnp.float32
I32 = jnp.int32
D = 6144
HALF = 3072
NG = 16
SLICE = 384
CAP = 10
ROWS = 160
MESH = pl.DeviceIdType.MESH


def iota(shape, dim):
    return lax.broadcasted_iota(I32, shape, dim)


def kernel(
    q_hbm, kn_hbm, vn_hbm, len_hbm, ids_hbm, lg_hbm,
    k_hbm, v_hbm, res_hbm, gain_hbm, wg_hbm, wu_hbm, wd_hbm,
    out_ref,
    q_ref, kn_ref, vn_ref, len_ref, ids_ref, lg_ref,
    k_v, v_v, res_v, gain_v,
    qs, res24, att24, sq_send, sq_recv, tok, wk, wd_r,
    agb, gu_send, gu_recv, hid_send, hid_recv,
    lr_send, lr_recv, fin_send, fin_recv,
    loc_sem, sq_sem, a_ss, a_rs, l_ss, l_rs, wk_ss, wk_rs, wd_ss, wd_rs,
    ag_ss, ag_rs, gu_sem, hid_ss, hid_rs, lr_ss, lr_rs, fin_ss, fin_rs,
):
    g = lax.axis_index("grp")
    d = lax.axis_index("dev")
    a = d // 8
    part = d % 8
    b = part // 2
    c = d % 2
    xg = g // 4
    yg = g % 4

    def did(gg, dd):
        return (gg, dd)

    def rc(src, dst, ss, rs, dev):
        return pltpu.make_async_remote_copy(
            src_ref=src, dst_ref=dst, send_sem=ss, recv_sem=rs,
            device_id=dev, device_id_type=MESH,
        )

    barrier = pltpu.get_barrier_semaphore()

    def sig(dev):
        pl.semaphore_signal(barrier, inc=1, device_id=dev, device_id_type=MESH)

    def fin_out(k):
        return 2 * part + k // 4, 4 * g + k % 4

    def fin_in(e):
        return d // 4, e * 8 + g // 2

    def is_me(gg, dd):
        return jnp.logical_and(gg == g, dd == d)

    agb[...] = jnp.zeros_like(agb)
    lr_recv[...] = jnp.zeros_like(lr_recv)
    tok[...] = jnp.zeros_like(tok)
    sig(did(g, ((a + 1) % 8) * 8 + part))
    sig(did(g, ((a + 7) % 8) * 8 + part))

    d_other = d + 1 - 2 * c

    def sig_line(k, x):
        sig(did(g, a * 8 + ((b + k) % 4) * 2 + c))
        return x

    lax.fori_loop(1, 4, sig_line, 0)

    def sig_xy(k, x):
        sig(did((g + k) % NG, d))
        return x

    lax.fori_loop(1, NG, sig_xy, 0)
    sig(did(g, d_other))

    half_at = pl.multiple_of(c * HALF, HALF)
    loads = [
        pltpu.make_async_copy(k_hbm, k_v, loc_sem.at[0]),
        pltpu.make_async_copy(v_hbm, v_v, loc_sem.at[1]),
        pltpu.make_async_copy(res_hbm.at[:, pl.ds(half_at, HALF)], res_v, loc_sem.at[2]),
        pltpu.make_async_copy(gain_hbm.at[pl.ds(pl.multiple_of(c * 24, 8), 24)], gain_v, loc_sem.at[3]),
    ]
    small = [
        pltpu.make_async_copy(src, dst, loc_sem.at[7 + i])
        for i, (src, dst) in enumerate([
            (q_hbm, q_ref), (len_hbm, len_ref), (kn_hbm, kn_ref), (vn_hbm, vn_ref),
            (ids_hbm, ids_ref), (lg_hbm, lg_ref)])
    ]
    for cp in small + loads:
        cp.start()

    token = d // 2
    for cp in small:
        cp.wait()
    length = len_ref[token]
    qs[...] = jnp.zeros_like(qs)
    q_row = q_ref[...].astype(F32)
    for i in range(24):
        qs[8 * (i // 6) + i % 6 : 8 * (i // 6) + i % 6 + 1, :] = q_row[:, 128 * i : 128 * i + 128]
    kn = kn_ref[...].astype(F32)
    vn = vn_ref[...].astype(F32)
    live = iota((8, 512), 1) < length
    scale = 128 ** (-0.5)
    loads[0].wait()
    loads[1].wait()
    for h in range(4):
        cols = slice(128 * h, 128 * h + 128)
        q_h = qs[8 * h : 8 * h + 8, :]
        s = lax.dot_general(
            q_h.astype(BF), k_v[:, cols], (((1,), (1,)), ((), ())), preferred_element_type=F32
        ) * scale
        s = jnp.where(live, s, -1e30)
        s_new = jnp.sum(q_h * kn[:, cols], axis=1, keepdims=True) * scale
        top = jnp.maximum(jnp.max(s, axis=1, keepdims=True), s_new)
        e = jnp.exp(s - top)
        e_new = jnp.exp(s_new - top)
        den = jnp.sum(e, axis=1, keepdims=True) + e_new
        o = jnp.dot((e / den).astype(BF), v_v[:, cols], preferred_element_type=F32)
        o = o + (e_new / den).astype(BF).astype(F32) * vn[:, cols]
        att24[6 * h : 6 * h + 6, :] = o[0:6, :].astype(BF).astype(F32)
    loads[2].wait()
    mine = iota((32, HALF), 0) == token
    res_row = jnp.sum(jnp.where(mine, res_v[...].astype(F32), 0.0), axis=0, keepdims=True)
    for i in range(24):
        res24[i : i + 1, :] = res_row[:, 128 * i : 128 * i + 128]
    summed = att24[...] + res24[...]
    sq = jnp.sum(jnp.sum(summed * summed, axis=1, keepdims=True), axis=0, keepdims=True)
    sq_send[...] = jnp.broadcast_to(sq, (8, 128))

    pl.semaphore_wait(barrier, 15 + 1 + 2 + 3)

    sq_copy = rc(sq_send, sq_recv, sq_sem.at[0], sq_sem.at[1], did(g, d_other))
    sq_copy.start()

    ids = ids_ref[...]
    id0, id1 = ids[0:1, :], ids[1:2, :]
    lg = lg_ref[...]
    l0, l1 = lg[0:1, :], lg[1:2, :]
    lm = jnp.maximum(l0, l1)
    e0, e1 = jnp.exp(l0 - lm), jnp.exp(l1 - lm)
    p0, p1 = e0 / (e0 + e1), e1 / (e0 + e1)
    before = jnp.where(iota((32, 32), 0) < iota((32, 32), 1), 1.0, 0.0).astype(BF)
    own = jnp.where(id0 == a, 1.0, 0.0) + jnp.where(id1 == a, 1.0, 0.0)
    own = jnp.broadcast_to(own, (16, 32))
    own_pos = jnp.dot(own.astype(BF), before, preferred_element_type=F32)
    pick_hot = jnp.where(own_pos == iota((16, 32), 0).astype(F32), own, 0.0)
    at = iota((32, 1024), 1)
    spread = jnp.where(iota((32, 1024), 0) == ((at // 32) % 8) * 4 + at // 256, 1.0, 0.0)
    pick_exp = jnp.dot(pick_hot.astype(BF), spread.astype(BF), preferred_element_type=F32)
    in_tok = iota((16, 1024), 1) % 32
    select = jnp.concatenate(
        [jnp.where(in_tok == j, pick_exp, 0.0).astype(BF) for j in range(24)], axis=0
    )

    loads[3].wait()
    sq_copy.wait_recv()
    total = sq_send[...] + sq_recv[...]
    inv = lax.rsqrt(total[0:1, 0:1] * (1.0 / D) + 1e-05)
    normed = summed * inv * gain_v[...]
    tok[b, a] = jnp.concatenate([normed, jnp.zeros((8, 128), F32)], axis=0).astype(BF)

    def tk(bb, aa):
        return tok.at[bb, aa, pl.ds(0, 24)]

    def a_copy(src_a, way, number):
        return rc(tk(b, src_a), tk(b, src_a), a_ss.at[number], a_rs.at[src_a],
                  did(g, ((a + way + 8) % 8) * 8 + part))

    def l_copy(k, bb, aa, to):
        return rc(tk(bb, aa), tk(bb, aa), l_ss.at[k, aa], l_rs.at[bb, aa], did(g, a * 8 + to * 2 + c))

    leaving = []

    def send(cp):
        cp.start()
        leaving.append(cp)

    def to_line(aa):
        for k in (1, 2, 3):
            send(l_copy(k, b, aa, (b + k) % 4))

    send(a_copy(a, 1, 0))
    send(a_copy(a, -1, 4))
    to_line(a)

    def cut(ref, gg):
        return ref.at[:, pl.ds(pl.multiple_of(SLICE * gg, 128), SLICE)]

    mine_half = pl.ds(half_at, HALF)
    other_half = pl.ds(pl.multiple_of((1 - c) * HALF, HALF), HALF)
    wk_copies = [
        rc(ref.at[:, other_half], wk.at[2 + i], wk_ss.at[i], wk_rs.at[i], did(g, d_other))
        for i, ref in enumerate((wg_hbm, wu_hbm))
    ]
    wk_own = [
        pltpu.make_async_copy(ref.at[:, mine_half], wk.at[i], loc_sem.at[4 + i])
        for i, ref in enumerate((wg_hbm, wu_hbm))
    ]

    def wd_copy(k, src_g, dst_g):
        return rc(
            cut(wd_hbm, dst_g), wd_r.at[src_g],
            wd_ss.at[k], wd_rs.at[src_g], did(dst_g, d))

    def reshard_down(k, x):
        wd_copy(k, g, (g + k) % NG).start()
        return x

    for cp in wk_copies + wk_own:
        cp.start()
    lax.fori_loop(1, NG, reshard_down, 0)
    wd_own = pltpu.make_async_copy(cut(wd_hbm, g), wd_r.at[g], loc_sem.at[6])
    wd_own.start()

    for i in (1, 2, 3, 4):
        left = (a - i + 8) % 8
        a_copy(left, 1, 0).wait_recv()
        if i < 4:
            send(a_copy(left, 1, i))
        to_line(left)
        if i < 4:
            right = (a + i) % 8
            a_copy(right, -1, 4).wait_recv()
            if i < 3:
                send(a_copy(right, -1, 4 + i))
            to_line(right)

    def l_arrive(i, x):
        k, aa = 1 + i // 8, i % 8
        bb = (b + k) % 4
        l_copy(k, bb, aa, bb).wait_recv()
        return x

    lax.fori_loop(0, 24, l_arrive, 0)

    picked = jnp.dot(select, tok[...].reshape(1024, 128), preferred_element_type=F32).astype(BF)
    agb[xg, yg] = picked.reshape(24, 16, 128)

    def side(p, du, dv):
        dx, dy = (du, dv) if p == 0 else (dv, du)
        return did(((xg + dx + 4) % 4) * 4 + (yg + dy + 4) % 4, d)

    def piece(p, du, dv, j, n):
        u, v = (xg, yg) if p == 0 else (yg, xg)
        u, v = (u + du + 4) % 4, (v + dv + 4) % 4
        js = pl.ds(12 * p + j, n)
        return agb.at[u, v, js, pl.ds(0, CAP)] if p == 0 else agb.at[v, u, js, pl.ds(0, CAP)]

    def first(p, off, j, n, way, number):
        ref = piece(p, off, 0, j, n)
        return rc(ref, ref, ag_ss.at[p, number], ag_rs.at[p, number], side(p, way, 0))

    offs = (0, -1, 1, 2)

    def second(p, which, off, j, n, way, number):
        ref = piece(p, offs[which], off, j, n)
        at_sem = 4 + 4 * which + number
        return rc(ref, ref, ag_ss.at[p, at_sem], ag_rs.at[p, at_sem], side(p, 0, way))

    def both_ways(p, which):
        send(second(p, which, 0, 0, 12, 1, 0))
        send(second(p, which, 0, 0, 12, -1, 1))

    def relay(p, which):
        second(p, which, -1, 0, 12, 1, 0).wait_recv()
        send(second(p, which, -1, 0, 6, 1, 2))
        second(p, which, 1, 0, 12, -1, 1).wait_recv()
        send(second(p, which, 1, 6, 6, -1, 3))

    for p in range(2):
        send(first(p, 0, 0, 12, 1, 0))
        send(first(p, 0, 0, 12, -1, 1))
    for p in range(2):
        both_ways(p, 0)
    for p in range(2):
        first(p, -1, 0, 12, 1, 0).wait_recv()
        send(first(p, -1, 0, 6, 1, 2))
        first(p, 1, 0, 12, -1, 1).wait_recv()
        send(first(p, 1, 6, 6, -1, 3))
        both_ways(p, 1)
        both_ways(p, 2)
    for p in range(2):
        relay(p, 0)
    for p in range(2):
        first(p, -2, 0, 6, 1, 2).wait_recv()
        first(p, 2, 6, 6, -1, 3).wait_recv()
        both_ways(p, 3)
    for which in (1, 2, 3):
        for p in range(2):
            relay(p, which)
    for which in range(4):
        for p in range(2):
            second(p, which, -2, 0, 6, 1, 2).wait_recv()
            second(p, which, 2, 6, 6, -1, 3).wait_recv()

    for cp in wk_own:
        cp.wait()
    for cp in wk_copies:
        cp.wait_recv()
    x_rows = jnp.concatenate([agb[:, :, j].reshape(256, 128) for j in range(24)], axis=1)
    y = lax.dot_general(
        x_rows, wk[...].reshape(256, HALF), (((1,), (1,)), ((), ())), preferred_element_type=F32
    )
    gu_send[...] = y[:, 128:]
    gu_copy = rc(gu_send, gu_recv, gu_sem.at[0], gu_sem.at[1], did(g, d_other))
    gu_copy.start()
    squeeze = jnp.where(
        iota((ROWS, 256), 1) == (iota((ROWS, 256), 0) // CAP) * 16 + iota((ROWS, 256), 0) % CAP, 1.0, 0.0
    ).astype(BF)
    gu_copy.wait_recv()
    both = y[:, :128] + gu_recv[...]
    gate, up = both[:, :64], both[:, 64:]
    hidden = (gate / (1.0 + jnp.exp(-gate)) * up).astype(BF)
    hidden = jnp.dot(squeeze, hidden, preferred_element_type=F32)
    hid_send[...] = jnp.concatenate([hidden[:80], hidden[80:]], axis=1).astype(BF)
    hid_recv[g] = hid_send[...]

    def hid_copy(k, src_g, dst_g):
        return rc(hid_send, hid_recv.at[src_g], hid_ss.at[k], hid_rs.at[src_g], did(dst_g, d))

    def hid_out(k, x):
        hid_copy(k, g, (g + k) % NG).start()
        return x

    lax.fori_loop(1, NG, hid_out, 0)
    wd_own.wait()

    def wd_in(k, x):
        wd_copy(k, (g + k) % NG, g).wait_recv()
        return x

    lax.fori_loop(1, NG, wd_in, 0)

    def hid_in(k, x):
        hid_copy(k, (g + k) % NG, g).wait_recv()
        return x

    lax.fori_loop(1, NG, hid_in, 0)
    tops, lows = [], []
    for i in range(8):
        h0, h1 = hid_recv[2 * i], hid_recv[2 * i + 1]
        tops.append(jnp.concatenate([h0[:, :64], h1[:, :64]], axis=1))
        lows.append(jnp.concatenate([h0[:, 64:], h1[:, 64:]], axis=1))
    hid_all = jnp.concatenate(
        [jnp.concatenate(tops, axis=1), jnp.concatenate(lows, axis=1)], axis=0
    )
    down = jnp.dot(hid_all, wd_r[...].reshape(1024, SLICE), preferred_element_type=F32).astype(BF)
    widen = jnp.where(
        jnp.logical_and(
            iota((256, ROWS), 1) == (iota((256, ROWS), 0) // 16) * CAP + iota((256, ROWS), 0) % 16,
            iota((256, ROWS), 0) % 16 < CAP,
        ), 1.0, 0.0,
    ).astype(BF)
    wide = jnp.dot(widen, down, preferred_element_type=F32).astype(BF)
    for j in range(3):
        lr_send[:, :, j] = wide[:, 128 * j : 128 * j + 128].reshape(8, 2, 16, 128)

    def lr_copy(k, src_p, dst_p, dev_p):
        return rc(lr_send.at[dst_p, :, :, pl.ds(0, CAP)], lr_recv.at[src_p, :, :, pl.ds(0, CAP)], lr_ss.at[k], lr_rs.at[src_p],
                  did(g, a * 8 + dev_p))

    for k in range(1, 8):
        lr_copy(k, part, (part + k) % 8, (part + k) % 8).start()
    lr_recv[part] = lr_send[part]
    for k in range(1, 8):
        pp = (part + k) % 8
        lr_copy(k, pp, part, pp).wait_recv()
    rows = jnp.sum(lr_recv[...].astype(F32), axis=0)
    halves = [jnp.concatenate([rows[i, j] for j in range(3)], axis=1) for i in range(2)]
    for k in range(8):
        block = halves[k // 4][:, 96 * (k % 4) : 96 * (k % 4) + 96]
        fin_send[k] = jnp.concatenate([block, jnp.zeros((16, 32), F32)], axis=1).astype(BF)

    def fin_go(k, x):
        go, do = fin_out(k)

        @pl.when(jnp.logical_not(is_me(go, do)))
        def _():
            rc(fin_send.at[k], fin_recv.at[a], fin_ss.at[k], fin_rs.at[a], did(go, do)).start()

        @pl.when(is_me(go, do))
        def _():
            fin_recv[a] = fin_send[k]

        return x

    lax.fori_loop(0, 8, fin_go, 0)

    slot = iota((128, 32), 0)
    hit0 = jnp.where(id0 == slot // 16, 1.0, 0.0)
    hit1 = jnp.where(id1 == slot // 16, 1.0, 0.0)
    hits = hit0 + hit1
    places = jnp.dot(hits.astype(BF), before, preferred_element_type=F32)
    combine = jnp.where(places == (slot % 16).astype(F32), hit0 * p0 + hit1 * p1, 0.0)

    def fin_come(e, x):
        gi, di = fin_in(e)

        @pl.when(jnp.logical_not(is_me(gi, di)))
        def _():
            rc(fin_send.at[0], fin_recv.at[e], fin_ss.at[e], fin_rs.at[e], did(gi, di)).wait_recv()

        return x

    lax.fori_loop(0, 8, fin_come, 0)
    result = lax.dot_general(
        combine, fin_recv[...].reshape(128, 128).astype(F32), (((0,), (0,)), ((), ())), precision=lax.Precision.HIGHEST,
        preferred_element_type=F32,
    )
    out_ref[...] = result[:, :96].astype(BF)

    sq_copy.wait_send()

    def xy_left(k, x):
        gg = (g + k) % NG
        wd_copy(k, g, gg).wait_send()
        hid_copy(k, g, gg).wait_send()
        return x

    lax.fori_loop(1, NG, xy_left, 0)

    for cp in leaving + wk_copies + [gu_copy]:
        cp.wait_send()
    for k in range(1, 8):
        lr_copy(k, part, (part + k) % 8, (part + k) % 8).wait_send()

    def fin_left(k, x):
        go, do = fin_out(k)

        @pl.when(jnp.logical_not(is_me(go, do)))
        def _():
            rc(fin_send.at[k], fin_recv.at[a], fin_ss.at[k], fin_rs.at[a], did(go, do)).wait_send()

        return x

    lax.fori_loop(0, 8, fin_left, 0)


def body(
    queries, cached_key_rows, cached_value_rows, incoming_keys, incoming_values, lengths,
    residual, norm_gain, expert_ids, route_logits, w_gate, w_up, w_down,
):
    vmem = pl.BlockSpec(memory_space=pltpu.VMEM)
    anyw = pl.BlockSpec(memory_space=pl.ANY)
    dma = pltpu.SemaphoreType.DMA
    return pl.pallas_call(
        kernel,
        out_shape=jax.ShapeDtypeStruct((32, 96), BF),
        in_specs=[anyw] * 13,
        out_specs=vmem,
        scratch_shapes=[
            pltpu.VMEM((1, HALF), BF),
            pltpu.VMEM((1, 512), BF),
            pltpu.VMEM((1, 512), BF),
            pltpu.SMEM((32,), I32),
            pltpu.VMEM((2, 32), I32),
            pltpu.VMEM((2, 32), F32),
            pltpu.VMEM((512, 512), BF),
            pltpu.VMEM((512, 512), BF),
            pltpu.VMEM((32, HALF), BF),
            pltpu.VMEM((24, 128), F32),
            pltpu.VMEM((32, 128), F32),
            pltpu.VMEM((24, 128), F32),
            pltpu.VMEM((24, 128), F32),
            pltpu.VMEM((8, 128), F32),
            pltpu.VMEM((8, 128), F32),
            pltpu.VMEM((4, 8, 32, 128), BF),
            pltpu.VMEM((4, 64, HALF), BF),
            pltpu.VMEM((NG, 64, SLICE), BF),
            pltpu.VMEM((4, 4, 24, 16, 128), BF),
            pltpu.VMEM((256, 128), F32),
            pltpu.VMEM((256, 128), F32),
            pltpu.VMEM((80, 128), BF),
            pltpu.VMEM((NG, 80, 128), BF),
            pltpu.VMEM((8, 2, 3, 16, 128), BF),
            pltpu.VMEM((8, 2, 3, 16, 128), BF),
            pltpu.VMEM((8, 16, 128), BF),
            pltpu.VMEM((8, 16, 128), BF),
            dma((13,)), dma((2,)), dma((8,)), dma((8,)), dma((4, 8)), dma((4, 8)),
            dma((2,)), dma((2,)), dma((NG,)), dma((NG,)),
            dma((2, 20)), dma((2, 20)), dma((2,)), dma((NG,)), dma((NG,)),
            dma((8,)), dma((8,)), dma((8,)), dma((8,)),
        ],
        compiler_params=pltpu.CompilerParams(
            collective_id=0, has_side_effects=True, vmem_limit_bytes=67000000
        ),
    )(
        queries, incoming_keys, incoming_values, lengths, expert_ids.T, route_logits.T,
        cached_key_rows.reshape(512, 512), cached_value_rows.reshape(512, 512), residual,
        norm_gain.reshape(48, 128), w_gate.T, w_up.T, w_down,
    )


def solution(mesh):
    return jax.shard_map(
        body,
        mesh=mesh,
        in_specs=(
            P(("grp", "dev"), None),
            P(("grp", "dev"), None, None),
            P(("grp", "dev"), None, None),
            P(("grp", "dev"), None),
            P(("grp", "dev"), None),
            P("grp"),
            P("grp", None),
            P(),
            P("grp", None),
            P("grp", None),
            P(None, ("dev", "grp")),
            P(None, ("dev", "grp")),
            P(("dev", "grp"), None),
        ),
        out_specs=P("grp", "dev"),
        check_vma=False,
    )
```

```python
import jax
import jax.numpy as jnp
from jax import lax
from jax.experimental import pallas as pl
from jax.experimental.pallas import tpu as pltpu
from jax.sharding import PartitionSpec as P

BF = jnp.bfloat16
F32 = jnp.float32
I32 = jnp.int32
D = 6144
HALF = 3072
NG = 16
SLICE = 384
CAP = 10
ROWS = 160
MESH = pl.DeviceIdType.MESH


def iota(shape, dim):
    return lax.broadcasted_iota(I32, shape, dim)


def kernel(
    q_hbm, kn_hbm, vn_hbm, len_hbm, ids_hbm, lg_hbm,
    k_hbm, v_hbm, res_hbm, gain_hbm, wg_hbm, wu_hbm, wd_hbm,
    out_ref,
    q_ref, kn_ref, vn_ref, len_ref, ids_ref, lg_ref,
    k_v, v_v, res_v, gain_v,
    qs, res24, att24, sq_send, sq_recv, tok, wk, wd_r,
    agb, gu_send, gu_recv, hid_send, hid_recv,
    lr_send, lr_recv, fin_send, fin_recv,
    loc_sem, sq_sem, a_ss, a_rs, l_ss, l_rs, wk_ss, wk_rs, wd_ss, wd_rs,
    ag_ss, ag_rs, gu_sem, hid_ss, hid_rs, lr_ss, lr_rs, fin_ss, fin_rs,
):
    g = lax.axis_index("grp")
    d = lax.axis_index("dev")
    a = d // 8
    part = d % 8
    b = part // 2
    c = d % 2
    xg = g // 4
    yg = g % 4

    def did(gg, dd):
        return (gg, dd)

    def rc(src, dst, ss, rs, dev):
        return pltpu.make_async_remote_copy(
            src_ref=src, dst_ref=dst, send_sem=ss, recv_sem=rs,
            device_id=dev, device_id_type=MESH,
        )

    barrier = pltpu.get_barrier_semaphore()

    def sig(dev):
        pl.semaphore_signal(barrier, inc=1, device_id=dev, device_id_type=MESH)

    def fin_out(k):
        return 2 * part + k // 4, 4 * g + k % 4

    def fin_in(e):
        return d // 4, e * 8 + g // 2

    def is_me(gg, dd):
        return jnp.logical_and(gg == g, dd == d)

    agb[...] = jnp.zeros_like(agb)
    lr_recv[...] = jnp.zeros_like(lr_recv)
    tok[...] = jnp.zeros_like(tok)
    sig(did(g, ((a + 1) % 8) * 8 + part))
    sig(did(g, ((a + 7) % 8) * 8 + part))

    d_other = d + 1 - 2 * c

    def sig_line(k, x):
        sig(did(g, a * 8 + ((b + k) % 4) * 2 + c))
        return x

    lax.fori_loop(1, 4, sig_line, 0)

    def sig_xy(k, x):
        sig(did((g + k) % NG, d))
        return x

    lax.fori_loop(1, NG, sig_xy, 0)
    sig(did(g, d_other))

    half_at = pl.multiple_of(c * HALF, HALF)
    loads = [
        pltpu.make_async_copy(k_hbm, k_v, loc_sem.at[0]),
        pltpu.make_async_copy(v_hbm, v_v, loc_sem.at[1]),
        pltpu.make_async_copy(res_hbm.at[:, pl.ds(half_at, HALF)], res_v, loc_sem.at[2]),
        pltpu.make_async_copy(gain_hbm.at[pl.ds(pl.multiple_of(c * 24, 8), 24)], gain_v, loc_sem.at[3]),
    ]
    small = [
        pltpu.make_async_copy(src, dst, loc_sem.at[7 + i])
        for i, (src, dst) in enumerate([
            (q_hbm, q_ref), (len_hbm, len_ref), (kn_hbm, kn_ref), (vn_hbm, vn_ref),
            (ids_hbm, ids_ref), (lg_hbm, lg_ref)])
    ]
    for cp in small + loads:
        cp.start()

    token = d // 2
    for cp in small:
        cp.wait()
    length = len_ref[token]
    qs[...] = jnp.zeros_like(qs)
    q_row = q_ref[...].astype(F32)
    for i in range(24):
        qs[8 * (i // 6) + i % 6 : 8 * (i // 6) + i % 6 + 1, :] = q_row[:, 128 * i : 128 * i + 128]
    kn = kn_ref[...].astype(F32)
    vn = vn_ref[...].astype(F32)
    live = iota((8, 512), 1) < length
    scale = 128 ** (-0.5)
    loads[0].wait()
    loads[1].wait()
    for h in range(4):
        cols = slice(128 * h, 128 * h + 128)
        q_h = qs[8 * h : 8 * h + 8, :]
        s = lax.dot_general(
            q_h.astype(BF), k_v[:, cols], (((1,), (1,)), ((), ())), preferred_element_type=F32
        ) * scale
        s = jnp.where(live, s, -1e30)
        s_new = jnp.sum(q_h * kn[:, cols], axis=1, keepdims=True) * scale
        top = jnp.maximum(jnp.max(s, axis=1, keepdims=True), s_new)
        e = jnp.exp(s - top)
        e_new = jnp.exp(s_new - top)
        den = jnp.sum(e, axis=1, keepdims=True) + e_new
        o = jnp.dot((e / den).astype(BF), v_v[:, cols], preferred_element_type=F32)
        o = o + (e_new / den).astype(BF).astype(F32) * vn[:, cols]
        att24[6 * h : 6 * h + 6, :] = o[0:6, :].astype(BF).astype(F32)
    loads[2].wait()
    mine = iota((32, HALF), 0) == token
    res_row = jnp.sum(jnp.where(mine, res_v[...].astype(F32), 0.0), axis=0, keepdims=True)
    for i in range(24):
        res24[i : i + 1, :] = res_row[:, 128 * i : 128 * i + 128]
    summed = att24[...] + res24[...]
    sq = jnp.sum(jnp.sum(summed * summed, axis=1, keepdims=True), axis=0, keepdims=True)
    sq_send[...] = jnp.broadcast_to(sq, (8, 128))

    pl.semaphore_wait(barrier, 15 + 1 + 2 + 3)

    sq_copy = rc(sq_send, sq_recv, sq_sem.at[0], sq_sem.at[1], did(g, d_other))
    sq_copy.start()

    ids = ids_ref[...]
    id0, id1 = ids[0:1, :], ids[1:2, :]
    lg = lg_ref[...]
    l0, l1 = lg[0:1, :], lg[1:2, :]
    lm = jnp.maximum(l0, l1)
    e0, e1 = jnp.exp(l0 - lm), jnp.exp(l1 - lm)
    p0, p1 = e0 / (e0 + e1), e1 / (e0 + e1)
    before = jnp.where(iota((32, 32), 0) < iota((32, 32), 1), 1.0, 0.0).astype(BF)
    own = jnp.where(id0 == a, 1.0, 0.0) + jnp.where(id1 == a, 1.0, 0.0)
    own = jnp.broadcast_to(own, (16, 32))
    own_pos = jnp.dot(own.astype(BF), before, preferred_element_type=F32)
    pick_hot = jnp.where(own_pos == iota((16, 32), 0).astype(F32), own, 0.0)
    at = iota((32, 1024), 1)
    spread = jnp.where(iota((32, 1024), 0) == ((at // 32) % 8) * 4 + at // 256, 1.0, 0.0)
    pick_exp = jnp.dot(pick_hot.astype(BF), spread.astype(BF), preferred_element_type=F32)
    in_tok = iota((16, 1024), 1) % 32
    select = jnp.concatenate(
        [jnp.where(in_tok == j, pick_exp, 0.0).astype(BF) for j in range(24)], axis=0
    )

    loads[3].wait()
    sq_copy.wait_recv()
    total = sq_send[...] + sq_recv[...]
    inv = lax.rsqrt(total[0:1, 0:1] * (1.0 / D) + 1e-05)
    normed = summed * inv * gain_v[...]
    tok[b, a] = jnp.concatenate([normed, jnp.zeros((8, 128), F32)], axis=0).astype(BF)

    def tk(bb, aa):
        return tok.at[bb, aa, pl.ds(0, 24)]

    def a_copy(src_a, way, number):
        return rc(tk(b, src_a), tk(b, src_a), a_ss.at[number], a_rs.at[src_a],
                  did(g, ((a + way + 8) % 8) * 8 + part))

    def l_copy(k, bb, aa, to):
        return rc(tk(bb, aa), tk(bb, aa), l_ss.at[k, aa], l_rs.at[bb, aa], did(g, a * 8 + to * 2 + c))

    leaving = []

    def send(cp):
        cp.start()
        leaving.append(cp)

    def to_line(aa):
        for k in (1, 2, 3):
            send(l_copy(k, b, aa, (b + k) % 4))

    send(a_copy(a, 1, 0))
    send(a_copy(a, -1, 4))
    to_line(a)

    def cut(ref, gg):
        return ref.at[:, pl.ds(pl.multiple_of(SLICE * gg, 128), SLICE)]

    mine_half = pl.ds(half_at, HALF)
    other_half = pl.ds(pl.multiple_of((1 - c) * HALF, HALF), HALF)
    wk_copies = [
        rc(ref.at[:, other_half], wk.at[2 + i], wk_ss.at[i], wk_rs.at[i], did(g, d_other))
        for i, ref in enumerate((wg_hbm, wu_hbm))
    ]
    wk_own = [
        pltpu.make_async_copy(ref.at[:, mine_half], wk.at[i], loc_sem.at[4 + i])
        for i, ref in enumerate((wg_hbm, wu_hbm))
    ]

    def wd_copy(k, src_g, dst_g):
        return rc(
            cut(wd_hbm, dst_g), wd_r.at[src_g],
            wd_ss.at[k], wd_rs.at[src_g], did(dst_g, d))

    def reshard_down(k, x):
        wd_copy(k, g, (g + k) % NG).start()
        return x

    for cp in wk_copies + wk_own:
        cp.start()
    lax.fori_loop(1, NG, reshard_down, 0)
    wd_own = pltpu.make_async_copy(cut(wd_hbm, g), wd_r.at[g], loc_sem.at[6])
    wd_own.start()

    for i in (1, 2, 3, 4):
        left = (a - i + 8) % 8
        a_copy(left, 1, 0).wait_recv()
        if i < 4:
            send(a_copy(left, 1, i))
        if i == 3:
            for k in (1, 2, 3):
                send(rc(tk(b, left), tk(b, left), l_ss.at[k, (a + 4) % 8], l_rs.at[b, left],
                        did(g, ((a + 1) % 8) * 8 + ((b + k) % 4) * 2 + c)))
        if i < 4:
            to_line(left)
        if i < 4:
            right = (a + i) % 8
            a_copy(right, -1, 4).wait_recv()
            if i < 3:
                send(a_copy(right, -1, 4 + i))
            to_line(right)

    def l_arrive(i, x):
        k, aa = 1 + i // 8, i % 8
        bb = (b + k) % 4
        l_copy(k, bb, aa, bb).wait_recv()
        return x

    lax.fori_loop(0, 24, l_arrive, 0)

    picked = jnp.dot(select, tok[...].reshape(1024, 128), preferred_element_type=F32).astype(BF)
    agb[xg, yg] = picked.reshape(24, 16, 128)

    def side(p, du, dv):
        dx, dy = (du, dv) if p == 0 else (dv, du)
        return did(((xg + dx + 4) % 4) * 4 + (yg + dy + 4) % 4, d)

    def piece(p, du, dv, j, n):
        u, v = (xg, yg) if p == 0 else (yg, xg)
        u, v = (u + du + 4) % 4, (v + dv + 4) % 4
        js = pl.ds(12 * p + j, n)
        return agb.at[u, v, js, pl.ds(0, CAP)] if p == 0 else agb.at[v, u, js, pl.ds(0, CAP)]

    def first(p, off, j, n, way, number):
        ref = piece(p, off, 0, j, n)
        return rc(ref, ref, ag_ss.at[p, number], ag_rs.at[p, number], side(p, way, 0))

    offs = (0, -1, 1, 2)

    def second(p, which, off, j, n, way, number):
        ref = piece(p, offs[which], off, j, n)
        at_sem = 4 + 4 * which + number
        return rc(ref, ref, ag_ss.at[p, at_sem], ag_rs.at[p, at_sem], side(p, 0, way))

    def both_ways(p, which):
        send(second(p, which, 0, 0, 12, 1, 0))
        send(second(p, which, 0, 0, 12, -1, 1))

    def relay(p, which):
        second(p, which, -1, 0, 12, 1, 0).wait_recv()
        send(second(p, which, -1, 0, 6, 1, 2))
        second(p, which, 1, 0, 12, -1, 1).wait_recv()
        send(second(p, which, 1, 6, 6, -1, 3))

    for p in range(2):
        send(first(p, 0, 0, 12, 1, 0))
        send(first(p, 0, 0, 12, -1, 1))
    for p in range(2):
        both_ways(p, 0)
    for p in range(2):
        first(p, -1, 0, 12, 1, 0).wait_recv()
        send(first(p, -1, 0, 6, 1, 2))
        first(p, 1, 0, 12, -1, 1).wait_recv()
        send(first(p, 1, 6, 6, -1, 3))
        both_ways(p, 1)
        both_ways(p, 2)
    for p in range(2):
        relay(p, 0)
    for p in range(2):
        first(p, -2, 0, 6, 1, 2).wait_recv()
        first(p, 2, 6, 6, -1, 3).wait_recv()
        both_ways(p, 3)
    for which in (1, 2, 3):
        for p in range(2):
            relay(p, which)
    for which in range(4):
        for p in range(2):
            second(p, which, -2, 0, 6, 1, 2).wait_recv()
            second(p, which, 2, 6, 6, -1, 3).wait_recv()

    for cp in wk_own:
        cp.wait()
    for cp in wk_copies:
        cp.wait_recv()
    x_rows = jnp.concatenate([agb[:, :, j].reshape(256, 128) for j in range(24)], axis=1)
    y = lax.dot_general(
        x_rows, wk[...].reshape(256, HALF), (((1,), (1,)), ((), ())), preferred_element_type=F32
    )
    gu_send[...] = y[:, 128:]
    gu_copy = rc(gu_send, gu_recv, gu_sem.at[0], gu_sem.at[1], did(g, d_other))
    gu_copy.start()
    squeeze = jnp.where(
        iota((ROWS, 256), 1) == (iota((ROWS, 256), 0) // CAP) * 16 + iota((ROWS, 256), 0) % CAP, 1.0, 0.0
    ).astype(BF)
    gu_copy.wait_recv()
    both = y[:, :128] + gu_recv[...]
    gate, up = both[:, :64], both[:, 64:]
    hidden = (gate / (1.0 + jnp.exp(-gate)) * up).astype(BF)
    hidden = jnp.dot(squeeze, hidden, preferred_element_type=F32)
    hid_send[...] = jnp.concatenate([hidden[:80], hidden[80:]], axis=1).astype(BF)
    hid_recv[g] = hid_send[...]

    def hid_copy(k, src_g, dst_g):
        return rc(hid_send, hid_recv.at[src_g], hid_ss.at[k], hid_rs.at[src_g], did(dst_g, d))

    steps = sorted(
        [(dx, dy) for dx in range(4) for dy in range(4) if dx or dy],
        key=lambda q: -min(q[0], 4 - q[0]) - min(q[1], 4 - q[1]))
    for k, (dx, dy) in enumerate(steps):
        send(hid_copy(k, g, ((xg + dx) % 4) * 4 + (yg + dy) % 4))
    wd_own.wait()

    def wd_in(k, x):
        wd_copy(k, (g + k) % NG, g).wait_recv()
        return x

    lax.fori_loop(1, NG, wd_in, 0)

    def hid_in(k, x):
        hid_copy(k, (g + k) % NG, g).wait_recv()
        return x

    lax.fori_loop(1, NG, hid_in, 0)
    tops, lows = [], []
    for i in range(8):
        h0, h1 = hid_recv[2 * i], hid_recv[2 * i + 1]
        tops.append(jnp.concatenate([h0[:, :64], h1[:, :64]], axis=1))
        lows.append(jnp.concatenate([h0[:, 64:], h1[:, 64:]], axis=1))
    hid_all = jnp.concatenate(
        [jnp.concatenate(tops, axis=1), jnp.concatenate(lows, axis=1)], axis=0
    )
    down = jnp.dot(hid_all, wd_r[...].reshape(1024, SLICE), preferred_element_type=F32).astype(BF)
    widen = jnp.where(
        jnp.logical_and(
            iota((256, ROWS), 1) == (iota((256, ROWS), 0) // 16) * CAP + iota((256, ROWS), 0) % 16,
            iota((256, ROWS), 0) % 16 < CAP,
        ), 1.0, 0.0,
    ).astype(BF)
    wide = jnp.dot(widen, down, preferred_element_type=F32).astype(BF)
    for j in range(3):
        lr_send[:, :, j] = wide[:, 128 * j : 128 * j + 128].reshape(8, 2, 16, 128)

    def lr_copy(k, src_p, dst_p, dev_p):
        return rc(lr_send.at[dst_p, :, :, pl.ds(0, CAP)], lr_recv.at[src_p, :, :, pl.ds(0, CAP)], lr_ss.at[k], lr_rs.at[src_p],
                  did(g, a * 8 + dev_p))

    for k in range(1, 8):
        lr_copy(k, part, (part + k) % 8, (part + k) % 8).start()
    lr_recv[part] = lr_send[part]
    for k in range(1, 8):
        pp = (part + k) % 8
        lr_copy(k, pp, part, pp).wait_recv()
    rows = jnp.sum(lr_recv[...].astype(F32), axis=0)
    halves = [jnp.concatenate([rows[i, j] for j in range(3)], axis=1) for i in range(2)]
    for k in range(8):
        block = halves[k // 4][:, 96 * (k % 4) : 96 * (k % 4) + 96]
        fin_send[k] = jnp.concatenate([block, jnp.zeros((16, 32), F32)], axis=1).astype(BF)

    def fin_go(k, x):
        go, do = fin_out(k)

        @pl.when(jnp.logical_not(is_me(go, do)))
        def _():
            rc(fin_send.at[k], fin_recv.at[a], fin_ss.at[k], fin_rs.at[a], did(go, do)).start()

        @pl.when(is_me(go, do))
        def _():
            fin_recv[a] = fin_send[k]

        return x

    lax.fori_loop(0, 8, fin_go, 0)

    slot = iota((128, 32), 0)
    hit0 = jnp.where(id0 == slot // 16, 1.0, 0.0)
    hit1 = jnp.where(id1 == slot // 16, 1.0, 0.0)
    hits = hit0 + hit1
    places = jnp.dot(hits.astype(BF), before, preferred_element_type=F32)
    combine = jnp.where(places == (slot % 16).astype(F32), hit0 * p0 + hit1 * p1, 0.0)

    def fin_come(e, x):
        gi, di = fin_in(e)

        @pl.when(jnp.logical_not(is_me(gi, di)))
        def _():
            rc(fin_send.at[0], fin_recv.at[e], fin_ss.at[e], fin_rs.at[e], did(gi, di)).wait_recv()

        return x

    lax.fori_loop(0, 8, fin_come, 0)
    result = lax.dot_general(
        combine, fin_recv[...].reshape(128, 128).astype(F32), (((0,), (0,)), ((), ())), precision=lax.Precision.HIGHEST,
        preferred_element_type=F32,
    )
    out_ref[...] = result[:, :96].astype(BF)

    sq_copy.wait_send()

    def xy_left(k, x):
        gg = (g + k) % NG
        wd_copy(k, g, gg).wait_send()
        return x

    lax.fori_loop(1, NG, xy_left, 0)

    for cp in leaving + wk_copies + [gu_copy]:
        cp.wait_send()
    for k in range(1, 8):
        lr_copy(k, part, (part + k) % 8, (part + k) % 8).wait_send()

    def fin_left(k, x):
        go, do = fin_out(k)

        @pl.when(jnp.logical_not(is_me(go, do)))
        def _():
            rc(fin_send.at[k], fin_recv.at[a], fin_ss.at[k], fin_rs.at[a], did(go, do)).wait_send()

        return x

    lax.fori_loop(0, 8, fin_left, 0)


def body(
    queries, cached_key_rows, cached_value_rows, incoming_keys, incoming_values, lengths,
    residual, norm_gain, expert_ids, route_logits, w_gate, w_up, w_down,
):
    vmem = pl.BlockSpec(memory_space=pltpu.VMEM)
    anyw = pl.BlockSpec(memory_space=pl.ANY)
    dma = pltpu.SemaphoreType.DMA
    return pl.pallas_call(
        kernel,
        out_shape=jax.ShapeDtypeStruct((32, 96), BF),
        in_specs=[anyw] * 13,
        out_specs=vmem,
        scratch_shapes=[
            pltpu.VMEM((1, HALF), BF),
            pltpu.VMEM((1, 512), BF),
            pltpu.VMEM((1, 512), BF),
            pltpu.SMEM((32,), I32),
            pltpu.VMEM((2, 32), I32),
            pltpu.VMEM((2, 32), F32),
            pltpu.VMEM((512, 512), BF),
            pltpu.VMEM((512, 512), BF),
            pltpu.VMEM((32, HALF), BF),
            pltpu.VMEM((24, 128), F32),
            pltpu.VMEM((32, 128), F32),
            pltpu.VMEM((24, 128), F32),
            pltpu.VMEM((24, 128), F32),
            pltpu.VMEM((8, 128), F32),
            pltpu.VMEM((8, 128), F32),
            pltpu.VMEM((4, 8, 32, 128), BF),
            pltpu.VMEM((4, 64, HALF), BF),
            pltpu.VMEM((NG, 64, SLICE), BF),
            pltpu.VMEM((4, 4, 24, 16, 128), BF),
            pltpu.VMEM((256, 128), F32),
            pltpu.VMEM((256, 128), F32),
            pltpu.VMEM((80, 128), BF),
            pltpu.VMEM((NG, 80, 128), BF),
            pltpu.VMEM((8, 2, 3, 16, 128), BF),
            pltpu.VMEM((8, 2, 3, 16, 128), BF),
            pltpu.VMEM((8, 16, 128), BF),
            pltpu.VMEM((8, 16, 128), BF),
            dma((13,)), dma((2,)), dma((8,)), dma((8,)), dma((4, 8)), dma((4, 8)),
            dma((2,)), dma((2,)), dma((NG,)), dma((NG,)),
            dma((2, 20)), dma((2, 20)), dma((2,)), dma((NG,)), dma((NG,)),
            dma((8,)), dma((8,)), dma((8,)), dma((8,)),
        ],
        compiler_params=pltpu.CompilerParams(
            collective_id=0, has_side_effects=True, vmem_limit_bytes=67000000
        ),
    )(
        queries, incoming_keys, incoming_values, lengths, expert_ids.T, route_logits.T,
        cached_key_rows.reshape(512, 512), cached_value_rows.reshape(512, 512), residual,
        norm_gain.reshape(48, 128), w_gate.T, w_up.T, w_down,
    )


def solution(mesh):
    return jax.shard_map(
        body,
        mesh=mesh,
        in_specs=(
            P(("grp", "dev"), None),
            P(("grp", "dev"), None, None),
            P(("grp", "dev"), None, None),
            P(("grp", "dev"), None),
            P(("grp", "dev"), None),
            P("grp"),
            P("grp", None),
            P(),
            P("grp", None),
            P("grp", None),
            P(None, ("dev", "grp")),
            P(None, ("dev", "grp")),
            P(("dev", "grp"), None),
        ),
        out_specs=P("grp", "dev"),
        check_vma=False,
    )
```
